256 devices in a mesh: tm: 8 (over y_hi, x), stream: 32 (over y_lo, z, core).
Axes of the slice: x: 4, y: 4 (y_hi: 2, y_lo: 2; y = y_hi * 2 + y_lo), z: 8, core: 2. Of those that a mesh axis runs over, the one named last changes fastest.
Arguments:
- tokens: bfloat16 [32, 1024, 768], P('stream', 'tm'), may hold values from -6 to 6
- cotangent: bfloat16 [32, 1024, 768], P('stream', 'tm'), may hold values from -6 to 6
- decay: float32 [32, 1024, 24], P('stream', 'tm'), may hold values from 0.4 to 1, as said below
- in_w: bfloat16 [768, 3328], P('stream'), may hold values from -0.21875 to 0.21875
- out_w: bfloat16 [1536, 768], P('stream'), may hold values from -0.15625 to 0.15625
- conv_w: float32 [4, 1792], replicated, may hold values from -3 to 3
- dskip: float32 [24], replicated, may hold values from 0.5 to 2
- norm_w: float32 [1536], replicated, may hold values from 0.1 to 1.9
Outputs:
- out: bfloat16 [32, 1024, 768], P('stream', 'tm')
- grad_tokens: bfloat16 [32, 1024, 768], P('stream', 'tm')
- grad_out_t: float32 [768, 1536], P(('tm', 'stream'))
The draws below stay inside these ranges and needn't reach their ends.
Inputs may be any that keep to these rules, and one draw needn't show every extreme that they name: decay lies strictly between 0 and 1.
All inputs are finite; a program needn't handle non-finite values.
Results may differ from the reference program's by a relative error of at most 0.015.
Values may be sent and summed in bfloat16 or wider, within the bound.
No kernel may reach another device: no remote copies, remote signals or barrier semaphores. Data moves between devices by JAX's collectives and lax.ppermute only.
A program may use at most 128 MiB of HBM per device.

```python
import math
import jax
import jax.numpy as jnp
from jax import lax

D = 768
INNER = 1536
HEAD_TOTAL = 24
STATE = 128
CONV = 4
TOK_DEV = 128
STAY_LENGTH = 1024
STAY_COUNT = 32
PROJ = 3328
XBC = 1792


def draw_decay(key, part):
    key_frequency, key_portion, key_jaggedness, key_spike, key_level = jax.random.split(key, 5)
    rate_low = jnp.log(0.02 / STAY_LENGTH)
    rate_high = jnp.log(1.0 / 30.0)
    base_rate = jax.random.uniform(key_frequency, (STAY_COUNT, 1, HEAD_TOTAL), jnp.float32, rate_low, rate_high)
    shard_factor = jax.random.uniform(key_portion, (STAY_COUNT, STAY_LENGTH // TOK_DEV, 1, HEAD_TOTAL), jnp.float32, jnp.log(0.5), jnp.log(2.0))
    shard_factor = jnp.broadcast_to(shard_factor, (STAY_COUNT, STAY_LENGTH // TOK_DEV, TOK_DEV, HEAD_TOTAL)).reshape(STAY_COUNT, STAY_LENGTH, HEAD_TOTAL)
    roughness = jax.random.uniform(key_jaggedness, (STAY_COUNT, STAY_LENGTH, HEAD_TOTAL), jnp.float32, 0.5, 1.5)
    step_frequency = jnp.exp(base_rate + shard_factor) * roughness
    spike_events = jax.random.bernoulli(key_spike, 2.0 / STAY_LENGTH, (STAY_COUNT, STAY_LENGTH, 1))
    spike_depth = jax.random.uniform(key_level, (STAY_COUNT, STAY_LENGTH, HEAD_TOTAL), jnp.float32, 0.5, 0.8)
    return (jnp.where(spike_events, spike_depth, 1.0) * jnp.exp(-step_frequency)).astype(jnp.float32)


def levels(rng, dims, shards, smallest, top_value):
    factor_of, own = 1.0, jax.random.fold_in(rng, 6)
    for position, shards_of in shards:
        steps = jnp.exp(jax.random.uniform(jax.random.fold_in(own, position), (shards_of,), jnp.float32, smallest / len(shards), top_value / len(shards)))
        factor_of = factor_of * jnp.repeat(steps, dims[position] // shards_of).reshape([-1 if axis == position else 1 for axis in range(len(dims))])
    return factor_of


def centred(own_key, dims, width, most, cuts=(), dtype=jnp.bfloat16):
    values = width * jax.random.normal(own_key, dims, jnp.float32)
    if cuts:
        values = values * levels(own_key, dims, cuts, -0.22, 0.18)
    return jnp.clip(values, -most, most).astype(dtype)


def setup_inputs(seed: int = 0) -> dict:
    keys = jax.random.split(jax.random.key(seed), 9)
    return {
        "tokens": centred(keys[0], (STAY_COUNT, STAY_LENGTH, D), 1.0, 6.0, ((0, 32), (1, 8))),
        "cotangent": centred(keys[1], (STAY_COUNT, STAY_LENGTH, D), 1.0, 6.0, ((0, 32), (1, 8))),
        "decay": draw_decay(jax.random.fold_in(keys[8], 71), 0),
        "in_w": centred(keys[3], (D, PROJ), D ** -0.5, 0.21875, ((0, 32),)),
        "out_w": centred(keys[4], (INNER, D), INNER ** -0.5, 0.15625, ((0, 32),)),
        "conv_w": centred(keys[5], (CONV, XBC), CONV ** -0.5, 3.0, (), jnp.float32),
        "dskip": jnp.clip(jnp.exp(jax.random.uniform(keys[6], (HEAD_TOTAL,), jnp.float32, math.log(0.5), math.log(2.0))), 0.5, 2.0),
        "norm_w": jnp.clip(1.0 + 0.18 * jax.random.normal(keys[7], (INNER,), jnp.float32), 0.1, 1.9),
    }


block_len = 128
highest = lax.Precision.HIGHEST

def conv_apply(extended, conv_weight):
    conv_taps = conv_weight.shape[0]
    row_count = extended.shape[0] - conv_taps + 1
    result = jnp.zeros((row_count, extended.shape[1]), jnp.float32)
    for offset in range(conv_taps):
        result = result + conv_weight[offset] * extended[offset:offset + row_count]
    return result

def block_ssm(carry_state, x_block, b_block, c_block, decay_log):
    cumulative = jnp.cumsum(decay_log, axis=0)
    carried = jnp.exp(cumulative)[:, :, None] * jnp.einsum('tn,hpn->thp', c_block, carry_state, precision=highest)
    scores = jnp.einsum('tn,sn->ts', c_block, b_block, precision=highest)
    later_idx = lax.broadcasted_iota(jnp.int32, scores.shape, 0)
    earlier_idx = lax.broadcasted_iota(jnp.int32, scores.shape, 1)
    causal = (later_idx >= earlier_idx)[:, :, None]
    log_gap = cumulative[:, None, :] - cumulative[None, :, :]
    weight = jnp.where(causal, jnp.exp(jnp.where(causal, log_gap, 0.0)), 0.0) * scores[:, :, None]
    inside = jnp.einsum('tsh,shp->thp', weight, x_block, precision=highest)
    fade_out = jnp.exp(cumulative[-1][None, :] - cumulative)
    added = jnp.einsum('shp,sn->hpn', fade_out[:, :, None] * x_block, b_block, precision=highest)
    carry_state = jnp.exp(cumulative[-1])[:, None, None] * carry_state + added
    return (carried + inside, carry_state)

def local_scan(conv_out, decay_log, skip_gain, head_count, state_width):
    row_count = conv_out.shape[0]
    inner_width = conv_out.shape[1] - 2 * state_width
    head_dim = inner_width // head_count
    block_rows = min(block_len, row_count)
    blocks = row_count // block_rows
    x_all = conv_out[:, :inner_width].reshape(blocks, block_rows, head_count, head_dim)
    b_all = conv_out[:, inner_width:inner_width + state_width].reshape(blocks, block_rows, state_width)
    c_all = conv_out[:, inner_width + state_width:].reshape(blocks, block_rows, state_width)
    d_all = decay_log.reshape(blocks, block_rows, head_count)

    def advance(carry_state, pieces):
        outputs, carry_state = block_ssm(carry_state, pieces[0], pieces[1], pieces[2], pieces[3])
        return (carry_state, outputs)
    start_state = jnp.zeros((head_count, head_dim, state_width), jnp.float32)
    final_state, results = lax.scan(advance, start_state, (x_all, b_all, c_all, d_all))
    x_heads = conv_out[:, :inner_width].reshape(row_count, head_count, head_dim)
    outputs = results.reshape(row_count, head_count, head_dim) + skip_gain[None, :, None] * x_heads
    return (outputs.reshape(row_count, inner_width), final_state)

def gate_norm(ssm_out, gate_in, norm_gain):
    gated = ssm_out * jax.nn.silu(gate_in)
    factor = lax.rsqrt(lax.optimization_barrier(jnp.mean(gated * gated, axis=-1, keepdims=True)) + 1e-05)
    return gated * factor * norm_gain

def stay_pass(inputs, grad_out, decay_row, in_w, out_w, conv_w, dskip, norm_w):
    projected = jnp.dot(inputs, in_w, preferred_element_type=jnp.float32).astype(jnp.bfloat16)
    gate_in = projected[:, :INNER].astype(jnp.float32)
    mix_in = projected[:, INNER:].astype(jnp.float32)
    extended = jnp.concatenate([jnp.zeros((CONV - 1, XBC), jnp.float32), mix_in], axis=0)
    pre_act, conv_back = jax.vjp(lambda values: conv_apply(values, conv_w), extended)
    conv_low = jax.nn.silu(pre_act).astype(jnp.bfloat16)
    conv_out = lax.optimization_barrier(conv_low).astype(jnp.float32)
    decay_log = jnp.log(decay_row)
    ssm_out, ssm_back = jax.vjp(lambda values: local_scan(values, decay_log, dskip, HEAD_TOTAL, STATE)[0], conv_out)
    normed, norm_back = jax.vjp(lambda first, second: gate_norm(first, second, norm_w), ssm_out, gate_in)
    normed_low = normed.astype(jnp.bfloat16)
    result = jnp.dot(normed_low, out_w, preferred_element_type=jnp.float32).astype(jnp.bfloat16)
    grad_normed = jnp.dot(grad_out, out_w.T, preferred_element_type=jnp.float32)
    grad_ssm, grad_gate = norm_back(grad_normed)
    grad_conv, = ssm_back(grad_ssm)
    sigmoid_pre = jax.nn.sigmoid(pre_act)
    grad_ext, = conv_back(grad_conv * sigmoid_pre * (1.0 + pre_act * (1.0 - sigmoid_pre)))
    grad_proj = jnp.concatenate([grad_gate, grad_ext[CONV - 1:]], axis=1).astype(jnp.bfloat16)
    grad_tokens = jnp.dot(grad_proj, in_w.T, preferred_element_type=jnp.float32).astype(jnp.bfloat16)
    grad_outw = jnp.dot(grad_out.T, normed_low, preferred_element_type=jnp.float32)
    return (result, grad_tokens, grad_outw)

def reference(tokens, cotangent, decay, in_w, out_w, conv_w, dskip, norm_w):

    def per_stay(carry, items):
        result, grad_tokens, grad_outw = stay_pass(items[0], items[1], items[2], in_w, out_w, conv_w, dskip, norm_w)
        return (carry + grad_outw, (result, grad_tokens))
    start = jnp.zeros((D, INNER), jnp.float32)
    sums, stacked = lax.scan(per_stay, start, (tokens, cotangent, decay))
    grad_scale = (STAY_COUNT * STAY_LENGTH) ** (-0.5)
    return (stacked[0], stacked[1], sums * grad_scale)
```

```python
import functools

import jax
import jax.numpy as jnp
from jax import lax
from jax.experimental import pallas as pl
from jax.experimental.pallas import tpu as pltpu
from jax.sharding import PartitionSpec as P

bf16, f32 = jnp.bfloat16, jnp.float32
CHUNK = 128
LANES = 128
XS = 4
NN = (((1,), (0,)), ((), ()))
NT = (((1,), (1,)), ((), ()))
TN = (((0,), (0,)), ((), ()))


def dot(a, b, dims=NN):
    return lax.dot_general(a.astype(bf16), b.astype(bf16), dims, preferred_element_type=f32)


def sig(v):
    return 1.0 / (1.0 + jnp.exp(-v))


def kernel_call(body, outs, *args, scratch=(), flops=10**8):
    spec = pl.BlockSpec(memory_space=pltpu.VMEM)
    size = sum(a.size * a.dtype.itemsize for a in args) + sum(
        o.size * o.dtype.itemsize for o in outs
    )
    return pl.pallas_call(
        body,
        out_shape=outs,
        in_specs=[spec] * len(args),
        out_specs=[spec] * len(outs),
        scratch_shapes=list(scratch),
        cost_estimate=pl.CostEstimate(flops=flops, bytes_accessed=size, transcendentals=0),
    )(*args)


def out(shape, dtype):
    return jax.ShapeDtypeStruct(shape, dtype)


def rows_of(c):
    return slice(c * CHUNK, (c + 1) * CHUNK)


def lanes_of(p):
    return slice(p * LANES, (p + 1) * LANES)


def halves():
    return lax.broadcasted_iota(jnp.int32, (CHUNK, LANES), 1) < LANES // 2


def causal():
    later = lax.broadcasted_iota(jnp.int32, (CHUNK, CHUNK), 0)
    return later >= lax.broadcasted_iota(jnp.int32, (CHUNK, CHUNK), 1)


def fades(cum_ref, cum_t_ref, c, head):
    column = cum_ref[rows_of(c), head * 64 : head * 64 + 1]
    row = cum_t_ref[head : head + 1, rows_of(c)]
    return jnp.where(causal(), jnp.exp(jnp.minimum(column - row, 0.0)), 0.0)


def project(tok, halo, w_in, conv_w, cum, gate, pre, conv, states, last, mix):
    width = gate.shape[1]
    chunks = gate.shape[0] // CHUNK
    mix[:8, :] = dot(halo[...], w_in[:, width:]).astype(bf16).astype(f32)
    state = jnp.zeros(last.shape, f32)
    for c in range(chunks):
        r = rows_of(c)
        gate[r, :] = dot(tok[r, :], w_in[:, :width]).astype(bf16)
        mix[8 + c * CHUNK : 8 + (c + 1) * CHUNK, :] = (
            dot(tok[r, :], w_in[:, width:]).astype(bf16).astype(f32)
        )
        for p in range(mix.shape[1] // LANES):
            s = lanes_of(p)
            value = jnp.zeros((CHUNK, LANES), f32)
            for k in range(4):
                start = 5 + k + c * CHUNK
                value = value + conv_w[k : k + 1, s] * mix[start : start + CHUNK, s]
            pre[r, s] = value
            conv[r, s] = (value * sig(value)).astype(bf16)
        states[c] = state
        end = cum[(c + 1) * CHUNK - 1 : (c + 1) * CHUNK, :]
        faded = jnp.exp(end - cum[r, :]) * conv[r, :width].astype(f32)
        state = jnp.exp(end) * state + dot(conv[r, width : width + 128], faded, TN)
    last[...] = state.astype(bf16)


def inside(conv, cum, cum_t, dskip, cot, w_out, norm_w, y, dn):
    width = y.shape[1]
    left = halves()
    for c in range(y.shape[0] // CHUNK):
        r = rows_of(c)
        b, cv = conv[r, width : width + 128], conv[r, width + 128 : width + 256]
        scores = dot(cv, b, NT)
        for p in range(width // LANES):
            s = lanes_of(p)
            x = conv[r, s].astype(f32)
            weight = jnp.concatenate(
                [fades(cum, cum_t, c, 2 * p) * scores, fades(cum, cum_t, c, 2 * p + 1) * scores],
                axis=1,
            )
            both = jnp.concatenate([jnp.where(left, x, 0.0), jnp.where(left, 0.0, x)], axis=0)
            y[r, s] = dot(weight, both) + dskip[:, s] * x
        dn[r, :] = dot(cot[r, :], w_out[...], NT) * norm_w[...]


def gated(conv, cum, states, entering, y_in, gate, dn, y, full, stats):
    width = y.shape[1]
    chunks = y.shape[0] // CHUNK
    carried = entering[...].astype(f32)
    ones = jnp.ones((8, width), f32)
    for c in range(chunks):
        r = rows_of(c)
        state = states[c] + carried
        full[c] = state.astype(bf16)
        carried = jnp.exp(cum[(c + 1) * CHUNK - 1 : (c + 1) * CHUNK, :]) * carried
        value = y_in[r, :] + jnp.exp(cum[r, :]) * dot(conv[r, width + 128 : width + 256], state)
        y[r, :] = value
        z = gate[r, :].astype(f32)
        g = value * z * sig(z)
        squares = lax.dot_general(
            ones, g * g, NT, precision=lax.Precision.HIGHEST, preferred_element_type=f32
        )
        cross = lax.dot_general(
            ones, g * dn[r, :], NT, precision=lax.Precision.HIGHEST, preferred_element_type=f32
        )
        stats[0:1, r] = squares[0:1]
        stats[1:2, r] = cross[0:1]


def normed_part(inner, y, gate, dn, sums, conv, cum, norm_w, cot, w_out, perm,
                part, dgate, dy, ends, first, dw, low):
    width = y.shape[1]
    chunks = y.shape[0] // CHUNK
    adjoint = jnp.zeros(first.shape, f32)
    for c in reversed(range(chunks)):
        r = rows_of(c)
        factor = lax.rsqrt(sums[r, 0:1] * (1.0 / inner) + 1e-05)
        lean = factor * factor * sums[r, 1:2] * (1.0 / inner)
        z = gate[r, :].astype(f32)
        q = sig(z)
        value = y[r, :]
        g = value * z * q
        low[r, :] = (g * factor * norm_w[...]).astype(bf16)
        dg = factor * (dn[r, :] - g * lean)
        dvalue = dg * z * q
        dy[r, :] = dvalue
        dgate[r, :] = (dg * value * q * (1.0 + z * (1.0 - q))).astype(bf16)
        part[r, :] = dot(low[r, :], w_out[...]).astype(bf16)
        ends[c] = adjoint
        end = cum[(c + 1) * CHUNK - 1 : (c + 1) * CHUNK, :]
        adjoint = jnp.exp(end) * adjoint + dot(
            conv[r, width + 128 : width + 256], jnp.exp(cum[r, :]) * dvalue, TN
        )
    first[...] = adjoint.astype(bf16)
    summed = dot(cot[...], low[...], TN)
    dw[...] = dot(perm[...], summed).astype(bf16)


def inside_back(conv, cum, cum_t, dskip, dy, dx, dbc):
    width = dy.shape[1]
    left = halves()
    for c in range(dy.shape[0] // CHUNK):
        r = rows_of(c)
        b, cv = conv[r, width : width + 128], conv[r, width + 128 : width + 256]
        scores = dot(cv, b, NT)
        dscores = jnp.zeros((CHUNK, CHUNK), f32)
        for p in range(width // LANES):
            s = lanes_of(p)
            x = conv[r, s]
            d = dy[r, s]
            da, db = jnp.where(left, d, 0.0), jnp.where(left, 0.0, d)
            fa, fb = fades(cum, cum_t, c, 2 * p), fades(cum, cum_t, c, 2 * p + 1)
            weight = jnp.concatenate([fa * scores, fb * scores], axis=0)
            dx[r, s] = dot(weight, jnp.concatenate([da, db], axis=0), TN) + dskip[:, s] * d
            dscores = dscores + fa * dot(da, x, NT) + fb * dot(db, x, NT)
        dbc[r, :128] = dot(dscores, cv, TN)
        dbc[r, 128:] = dot(dscores, b)


def conv_grad(conv, cum, full, ends, leaving, dy, dx, dbc, pre, gp, head):
    width = dy.shape[1]
    chunks = dy.shape[0] // CHUNK
    carried = leaving[...].astype(f32)
    for c in reversed(range(chunks)):
        r = rows_of(c)
        b = conv[r, width : width + 128]
        adjoint = ends[c] + carried
        end = cum[(c + 1) * CHUNK - 1 : (c + 1) * CHUNK, :]
        carried = jnp.exp(end) * carried
        fade = jnp.exp(end - cum[r, :])
        grad_x = dx[r, :] + fade * dot(b, adjoint)
        grad_b = dbc[r, :128] + dot(fade * conv[r, :width].astype(f32), adjoint, NT)
        grad_c = dbc[r, 128:] + dot(jnp.exp(cum[r, :]) * dy[r, :], full[c], NT)
        for lanes, grad in (
            (slice(0, width), grad_x),
            (slice(width, width + 128), grad_b),
            (slice(width + 128, width + 256), grad_c),
        ):
            v = pre[r, lanes]
            q = sig(v)
            gp[r, lanes] = grad * q * (1.0 + v * (1.0 - q))
    head[...] = gp[:8, :]


def token_grad(gp, after, conv_w, dgate, w_in, part, long):
    rows = gp.shape[0]
    width = dgate.shape[1]
    long[:rows, :] = gp[...]
    long[rows:, :] = after[...]
    for c in range(rows // CHUNK):
        r = rows_of(c)
        value = jnp.zeros((CHUNK, gp.shape[1]), f32)
        for k in range(4):
            start = c * CHUNK + 3 - k
            value = value + conv_w[k : k + 1, :] * long[start : start + CHUNK, :]
        part[r, :] = (
            dot(dgate[r, :], w_in[:, :width], NT) + dot(value, w_in[:, width:], NT)
        ).astype(bf16)


def shards(tokens, cotangent, decay, in_w, out_w, conv_w, dskip, norm_w):
    tm, stream = lax.axis_size("tm"), lax.axis_size("stream")
    me_t, me_s = lax.axis_index("tm"), lax.axis_index("stream")
    mine = lax.rem(me_t, XS)
    core = lax.rem(me_s, 2)
    heads = dskip.shape[0]
    inner = norm_w.shape[0]
    model = tokens.shape[2]
    state = (in_w.shape[1] - 2 * inner) // 2
    part_heads, width = heads // XS, inner // XS
    rows = XS * tokens.shape[1]
    x_groups = [[h * XS + i for i in range(XS)] for h in range(tm // XS)]
    up = [(i, i + XS) for i in range(XS)]
    down = [(i + XS, i) for i in range(XS)]

    def own(array, axis, size):
        return lax.dynamic_slice_in_dim(array, mine * size, size, axis)

    def swap_x(array):
        return lax.all_to_all(array, "tm", 0, 0, tiled=True, axis_index_groups=x_groups)

    def gather_x(array):
        return swap_x(jnp.broadcast_to(array[None], (XS,) + array.shape).reshape((-1,) + array.shape[1:]))

    piece = out_w.shape[0] // XS
    routes = []
    for t in range(tm):
        for s in range(stream):
            group, place = divmod(s, stream // XS)
            target = (t // XS * XS + group, XS * place + t % XS)
            routes.append((t * stream + s, target[0] * stream + target[1]))
    out_piece = lax.ppermute(own(out_w, 0, piece), ("tm", "stream"), routes)
    in_piece = jnp.concatenate(
        [own(in_w[:, :inner], 1, width), own(in_w[:, inner : 2 * inner], 1, width), in_w[:, 2 * inner :]],
        axis=1,
    )
    weights = jnp.concatenate([in_piece, out_piece.reshape(in_piece.shape[0], -1)], axis=1)

    halo = lax.ppermute(tokens[0, -8:], "tm", [(XS - 1, XS)])
    cores = [[i for i in range(stream) if i % 2 == c] for c in range(2)]
    half = stream // 2
    wide = jnp.broadcast_to(weights[None], (half,) + weights.shape)
    same = lax.all_to_all(wide, "stream", 0, 0, axis_index_groups=cores)
    other = lax.ppermute(same, "stream", [(i, i ^ 1) for i in range(stream)])
    even = jnp.where(core == 0, same, other)
    odd = jnp.where(core == 0, other, same)
    whole = jnp.stack([even, odd], axis=1).reshape(model, -1)
    w_in = whole[:, : in_piece.shape[1]]
    w_out = whole[:, in_piece.shape[1] :].reshape(width, model)

    both = gather_x(jnp.concatenate([tokens[0], cotangent[0], halo], axis=0))
    both = both.reshape(XS, -1, model)
    block = tokens.shape[1]
    tok = both[:, :block].reshape(rows, model)
    cot = both[:, block : 2 * block].reshape(rows, model)
    before = both[0, 2 * block :]
    cum_local = jnp.cumsum(jnp.log(decay[0]), axis=0).T.reshape(XS, part_heads, block)
    cum_all = swap_x(cum_local)
    cum_t = jnp.transpose(cum_all.reshape(XS, part_heads, block), (1, 0, 2)).reshape(part_heads, rows)
    cum = jnp.repeat(cum_t, width // part_heads, axis=0).T
    cum_t = jnp.concatenate([cum_t, jnp.zeros((8 - part_heads, rows), f32)], axis=0)
    taps = jnp.concatenate([own(conv_w[:, :inner], 1, width), conv_w[:, inner:]], axis=1)
    gain = own(norm_w, 0, width)[None]
    skip = jnp.repeat(own(dskip, 0, part_heads), width // part_heads)[None]
    mixed = width + 2 * state
    index = jnp.arange(model)
    source = index // 3 % tm * (3 * stream) + index // (3 * tm) * 3 + index % 3
    perm = (source[:, None] == index[None, :]).astype(bf16)

    gate, pre, conv, states, last = kernel_call(
        project,
        [out((rows, width), bf16), out((rows, mixed), f32), out((rows, mixed), bf16),
         out((rows // CHUNK, state, width), f32), out((state, width), bf16)],
        tok, before, w_in, taps, cum,
        scratch=[pltpu.VMEM((rows + 8, mixed), f32)],
    )
    entering = lax.ppermute(last, "tm", up)
    y_in, dn = kernel_call(
        inside,
        [out((rows, width), f32), out((rows, width), f32)],
        conv, cum, cum_t, skip, cot, w_out, gain,
    )
    y, full, stats = kernel_call(
        gated,
        [out((rows, width), f32), out(states.shape, bf16), out((2, rows), f32)],
        conv, cum, states, entering, y_in, gate, dn,
    )
    sums = gather_x(stats[None]).sum(axis=0).T
    part, dgate, dy, ends, first, dw = kernel_call(
        functools.partial(normed_part, inner),
        [out((rows, model), bf16), out((rows, width), bf16), out((rows, width), f32),
         out(states.shape, f32), out((state, width), bf16), out((model, width), bf16)],
        y, gate, dn, sums, conv, cum, gain, cot, w_out, perm,
        scratch=[pltpu.VMEM((rows, width), bf16)],
    )
    leaving = lax.ppermute(first, "tm", down)
    dx, dbc = kernel_call(
        inside_back,
        [out((rows, width), f32), out((rows, 2 * state), f32)],
        conv, cum, cum_t, skip, dy,
    )
    gp, head = kernel_call(
        conv_grad,
        [out((rows, mixed), f32), out((8, mixed), f32)],
        conv, cum, full, ends, leaving, dy, dx, dbc, pre,
    )
    after = lax.ppermute(head, "tm", down)
    (token_part,) = kernel_call(
        token_grad,
        [out((rows, model), bf16)],
        gp, after, taps, dgate, w_in,
        scratch=[pltpu.VMEM((rows + 8, mixed), f32)],
    )

    def collect(array):
        return swap_x(array).reshape(XS, block, model).astype(f32).sum(axis=0).astype(bf16)

    result = collect(part)
    grad_tokens = collect(token_part)
    pieces = lax.all_to_all(dw.reshape(stream, -1, width), "stream", 0, 0)
    summed = pieces.astype(f32).sum(axis=0).reshape(tm, 3, width)
    swapped = lax.all_to_all(summed, "tm", 0, 0).reshape(tm // XS, XS, 3, width).sum(axis=0)
    scale = (stream * tm * block) ** (-0.5)
    grad_out_t = jnp.transpose(swapped, (1, 0, 2)).reshape(3, inner) * scale
    return (result[None], grad_tokens[None], grad_out_t)


def solution(mesh):
    data = P("stream", "tm", None)
    in_specs = (data, data, data, P("stream", None), P("stream", None), P(), P(), P())
    out_specs = (data, data, P(("tm", "stream"), None))
    return jax.shard_map(shards, mesh=mesh, in_specs=in_specs, out_specs=out_specs, check_vma=False)
```

```python
import functools

import jax
import jax.numpy as jnp
from jax import lax
from jax.experimental import pallas as pl
from jax.experimental.pallas import tpu as pltpu
from jax.sharding import PartitionSpec as P


bf16, f32 = jnp.bfloat16, jnp.float32
CHUNK = 128
LANES = 128
LIMIT = None
XS = 4
NN = (((1,), (0,)), ((), ()))
NT = (((1,), (1,)), ((), ()))
TN = (((0,), (0,)), ((), ()))


def dot(a, b, dims=NN):
    return lax.dot_general(a.astype(bf16), b.astype(bf16), dims, preferred_element_type=f32)


def exact(a, b, dims=NN):
    return lax.dot_general(
        a, b, dims, precision=lax.Precision.HIGHEST, preferred_element_type=f32
    )


def sig(v):
    return 0.5 + 0.5 * jnp.tanh(0.5 * v)


def kernel_call(body, outs, *args, scalars=None, scratch=(), flops=10**8, limit=None):
    spec = pl.BlockSpec(memory_space=pltpu.VMEM)
    size = sum(a.size * a.dtype.itemsize for a in args) + sum(
        o.size * o.dtype.itemsize for o in outs
    )
    first = [] if scalars is None else [scalars]
    return pl.pallas_call(
        body,
        out_shape=outs,
        in_specs=[pl.BlockSpec(memory_space=pltpu.SMEM)] * len(first) + [spec] * len(args),
        out_specs=[spec] * len(outs),
        scratch_shapes=list(scratch),
        compiler_params=pltpu.CompilerParams(vmem_limit_bytes=limit or LIMIT),
        cost_estimate=pl.CostEstimate(flops=flops, bytes_accessed=size, transcendentals=0),
    )(*first, *args)


def out(shape, dtype):
    return jax.ShapeDtypeStruct(shape, dtype)


def rows_of(c):
    return slice(c * CHUNK, (c + 1) * CHUNK)


def lanes_of(p):
    return slice(p * LANES, (p + 1) * LANES)


def halves():
    return lax.broadcasted_iota(jnp.int32, (CHUNK, LANES), 1) < LANES // 2


def causal():
    later = lax.broadcasted_iota(jnp.int32, (CHUNK, CHUNK), 0)
    return later >= lax.broadcasted_iota(jnp.int32, (CHUNK, CHUNK), 1)


def fades(cum_ref, cum_t_ref, c, head):
    column = cum_ref[rows_of(c), head * 64 : head * 64 + 1]
    row = cum_t_ref[c, head : head + 1, :]
    return jnp.where(causal(), jnp.exp(jnp.minimum(column - row, 0.0)), 0.0)


def prepare(at, logs, in_w, tokens, cotangent, wide, gate_w, aux, send1, send2, send3, decays):
    width = gate_w.shape[1]
    inner = XS * width
    start = pl.multiple_of(at[0] * width, width)
    for i in range(wide.shape[0]):
        wide[i, :, :width] = in_w[:, pl.ds(inner + start, width)]
        wide[i, :, width:] = in_w[:, 2 * inner :]
    gate_w[...] = in_w[:, pl.ds(start, width)]
    block = logs.shape[1]
    step = lax.broadcasted_iota(jnp.int32, (block, block), 0)
    upto = (step <= lax.broadcasted_iota(jnp.int32, (block, block), 1)).astype(f32)
    cum = exact(jnp.log(logs[...]), upto)
    high = cum.astype(bf16).astype(f32)
    rest = cum - high
    middle = rest.astype(bf16).astype(f32)
    low = rest - middle
    per = logs.shape[0] // XS
    rest_rows = jnp.zeros((5, block), f32)
    for j in range(XS):
        for i in range(per):
            h = j * per + i
            rows = [high[h : h + 1], middle[h : h + 1], low[h : h + 1], rest_rows]
            decays[j, :, i * block : (i + 1) * block] = jnp.concatenate(rows, axis=0)
    aux[...] = decays[at[0]].astype(bf16)
    for r, send in enumerate((send1, send2, send3)):
        send[:block, :] = tokens[...]
        send[block : 2 * block, :] = cotangent[...]
        send[2 * block :, :] = decays[lax.rem(at[0] + r + 1, XS)].astype(bf16)


def assemble(at, same, other, target, lanes):
    own_first = at[1] == 0
    for i in range(same.shape[0]):
        a, b = same[i, :, lanes], other[i, :, lanes]
        target[48 * i : 48 * i + 24, :] = jnp.where(own_first, a, b).astype(target.dtype)
        target[48 * i + 24 : 48 * i + 48, :] = jnp.where(own_first, b, a).astype(target.dtype)


def project(at, tokens, cotangent, aux, recv1, recv2, recv3, halo, same, other, conv_w,
            tok, cot, w_mix, cum, cum_t, pre, conv, states, last, mix):
    width = last.shape[1]
    chunks = XS
    block = CHUNK
    assemble(at, same, other, w_mix, slice(None))
    for r, source in enumerate((None, recv1, recv2, recv3)):
        c = lax.rem(at[0] + (XS - r), XS)
        here = pl.ds(pl.multiple_of(c * block, block), block)
        if source is None:
            t, k, extra = tokens[...], cotangent[...], aux[...].astype(f32)
        else:
            t, k = source[:block, :], source[block : 2 * block, :]
            extra = source[2 * block :, :].astype(f32)
        tok[here, :] = t
        cot[here, :] = k
        mix[pl.ds(pl.multiple_of(8 + c * block, 8), block), :] = (
            dot(t, w_mix[...]).astype(bf16).astype(f32)
        )
        total = extra[0:1] + extra[1:2] + extra[2:3]
        heads = [total[:, i * block : (i + 1) * block] for i in range(width // 64)]
        cum_t[c] = jnp.concatenate(heads + [jnp.zeros((8 - len(heads), block), f32)], axis=0)
    mix[:8, :] = dot(halo[...], w_mix[...]).astype(bf16).astype(f32)
    left = halves()
    state = jnp.zeros(last.shape, f32)
    for c in range(chunks):
        r = rows_of(c)
        square = jnp.concatenate([cum_t[c], jnp.zeros((block - 8, block), f32)], axis=0).T
        for p in range(width // LANES):
            cum[r, lanes_of(p)] = jnp.where(
                left, square[:, 2 * p : 2 * p + 1], square[:, 2 * p + 1 : 2 * p + 2]
            )
        for p in range(mix.shape[1] // LANES):
            s = lanes_of(p)
            value = jnp.zeros((CHUNK, LANES), f32)
            for k in range(4):
                start = 5 + k + c * CHUNK
                value = value + conv_w[k : k + 1, s] * mix[start : start + CHUNK, s]
            pre[r, s] = value
            conv[r, s] = (value * sig(value)).astype(bf16)
        states[c] = state
        end = cum[(c + 1) * CHUNK - 1 : (c + 1) * CHUNK, :]
        faded = jnp.exp(end - cum[r, :]) * conv[r, :width].astype(f32)
        state = jnp.exp(end) * state + dot(conv[r, width : width + 128], faded, TN)
    last[...] = state.astype(bf16)


def inside(conv, cum, cum_t, dskip, y):
    width = y.shape[1]
    left = halves()
    for c in range(y.shape[0] // CHUNK):
        r = rows_of(c)
        b, cv = conv[r, width : width + 128], conv[r, width + 128 : width + 256]
        scores = dot(cv, b, NT)
        for p in range(width // LANES):
            s = lanes_of(p)
            x = conv[r, s].astype(f32)
            weight = jnp.concatenate(
                [fades(cum, cum_t, c, 2 * p) * scores, fades(cum, cum_t, c, 2 * p + 1) * scores],
                axis=1,
            )
            both = jnp.concatenate([jnp.where(left, x, 0.0), jnp.where(left, 0.0, x)], axis=0)
            y[r, s] = dot(weight, both) + dskip[:, s] * x


def gated(at, conv, cum, states, entering, y_in, tok, cot, same, other, norm_w,
          y, full, gate, dn, part, stats, w_gate, raw, w_out):
    width = y.shape[1]
    chunks = y.shape[0] // CHUNK
    assemble(at, same, other, w_gate, slice(0, width))
    for p in range(width // LANES):
        assemble(at, same, other, raw.at[p], slice(width + p * LANES, width + (p + 1) * LANES))
        for k in range(2):
            lanes = slice(k * width + p * LANES, k * width + (p + 1) * LANES)
            w_out[:, lanes] = raw[p, pl.ds(k, width, stride=2), :].astype(bf16)
    carried = entering[...].astype(f32)
    ones = jnp.ones((8, LANES), f32)
    for c in range(chunks):
        r = rows_of(c)
        gate[r, :] = dot(tok[r, :], w_gate[...]).astype(bf16)
        dn[r, :] = dot(cot[r, :], w_out[...], NT) * norm_w[...]
        state = states[c] + carried
        full[c] = state.astype(bf16)
        carried = jnp.exp(cum[(c + 1) * CHUNK - 1 : (c + 1) * CHUNK, :]) * carried
        value = y_in[r, :] + jnp.exp(cum[r, :]) * dot(conv[r, width + 128 : width + 256], state)
        y[r, :] = value
        z = gate[r, :].astype(f32)
        g = value * z * sig(z)
        part[c] = dot(g * norm_w[...], w_out[...]).astype(bf16)
        squares, cross = g * g, g * dn[r, :]
        squares = sum(squares[:, lanes_of(p)] for p in range(width // LANES))
        cross = sum(cross[:, lanes_of(p)] for p in range(width // LANES))
        stats[0:1, r] = exact(ones, squares, NT)[0:1]
        stats[1:2, r] = exact(ones, cross, NT)[0:1]


def normed_part(inner, y, gate, dn, stats0, stats1, stats2, stats3, conv, cum, norm_w, cot, perm,
                factors, dgate, dy, ends, first, dw, low):
    width = y.shape[1]
    chunks = y.shape[0] // CHUNK
    adjoint = jnp.zeros(first.shape, f32)
    for c in reversed(range(chunks)):
        r = rows_of(c)
        sums = stats0[:, r] + stats1[:, r] + stats2[:, r] + stats3[:, r]
        sums = jnp.concatenate([sums, jnp.zeros((CHUNK - 2, CHUNK), f32)], axis=0).T
        factor = lax.rsqrt(sums[:, 0:1] * (1.0 / inner) + 1e-05)
        lean = factor * factor * sums[:, 1:2] * (1.0 / inner)
        factors[c] = jnp.broadcast_to(factor, (CHUNK, LANES))
        z = gate[r, :].astype(f32)
        q = sig(z)
        value = y[r, :]
        g = value * z * q
        low[r, :] = (g * factor * norm_w[...]).astype(bf16)
        dg = factor * (dn[r, :] - g * lean)
        dvalue = dg * z * q
        dy[r, :] = dvalue
        dgate[r, :] = (dg * value * q * (1.0 + z * (1.0 - q))).astype(bf16)
        ends[c] = adjoint
        end = cum[(c + 1) * CHUNK - 1 : (c + 1) * CHUNK, :]
        adjoint = jnp.exp(end) * adjoint + dot(
            conv[r, width + 128 : width + 256], jnp.exp(cum[r, :]) * dvalue, TN
        )
    first[...] = adjoint.astype(bf16)
    summed = dot(cot[...], low[...], TN)
    dw[...] = dot(perm[...], summed).astype(bf16)


def inside_back(conv, cum, cum_t, dskip, dy, full, ends, pre, dx, dbc, head):
    width = dy.shape[1]
    left = halves()
    for c in range(dy.shape[0] // CHUNK):
        r = rows_of(c)
        b, cv = conv[r, width : width + 128], conv[r, width + 128 : width + 256]
        scores = dot(cv, b, NT)
        dscores = jnp.zeros((CHUNK, CHUNK), f32)
        for p in range(width // LANES):
            s = lanes_of(p)
            x = conv[r, s]
            d = dy[r, s]
            da, db = jnp.where(left, d, 0.0), jnp.where(left, 0.0, d)
            fa, fb = fades(cum, cum_t, c, 2 * p), fades(cum, cum_t, c, 2 * p + 1)
            weight = jnp.concatenate([fa * scores, fb * scores], axis=0)
            dx[r, s] = dot(weight, jnp.concatenate([da, db], axis=0), TN) + dskip[:, s] * d
            dscores = dscores + fa * dot(da, x, NT) + fb * dot(db, x, NT)
        dbc[r, :128] = dot(dscores, cv, TN)
        dbc[r, 128:] = dot(dscores, b)
    first = conv_rows(conv, cum, full[0], ends[0], dy, dx, dbc, pre, 0, 16)
    for lanes, value in first:
        head[:, lanes] = value[:8]


def conv_rows(conv, cum, state, adjoint, dy, dx, dbc, pre, start, count):
    width = dy.shape[1]
    r = slice(start, start + count)
    chunk_end = start // CHUNK * CHUNK + CHUNK
    fade = jnp.exp(cum[chunk_end - 1 : chunk_end, :] - cum[r, :])
    grad_x = dx[r, :] + fade * dot(conv[r, width : width + 128], adjoint)
    grad_b = dbc[r, :128] + dot(fade * conv[r, :width].astype(f32), adjoint, NT)
    grad_c = dbc[r, 128:] + dot(jnp.exp(cum[r, :]) * dy[r, :], state, NT)
    result = []
    for lanes, grad in (
        (slice(0, width), grad_x),
        (slice(width, width + 128), grad_b),
        (slice(width + 128, width + 256), grad_c),
    ):
        v = pre[r, lanes]
        q = sig(v)
        result.append((lanes, grad * q * (1.0 + v * (1.0 - q))))
    return result


def conv_grad(at, conv, cum, full, ends, leaving, dy, dx, dbc, pre, parts, factors, gp, result):
    chunks = dy.shape[0] // CHUNK
    carried = leaving[...].astype(f32)
    for c in reversed(range(chunks)):
        adjoint = ends[c] + carried
        end = cum[(c + 1) * CHUNK - 1 : (c + 1) * CHUNK, :]
        carried = jnp.exp(end) * carried
        rows = conv_rows(conv, cum, full[c], adjoint, dy, dx, dbc, pre, c * CHUNK, CHUNK)
        for lanes, value in rows:
            gp[rows_of(c), lanes] = value
    factor = factors[at[0]]
    for p in range(result.shape[1] // LANES):
        s = lanes_of(p)
        total = sum(parts[k, :, s].astype(f32) for k in range(XS))
        result[:, s] = (total * factor).astype(bf16)


def token_grad(at, gp, after, conv_w, dgate, w_gate, w_mix, own, to1, to2, to3, long, low):
    rows = gp.shape[0]
    long[:rows, :] = gp[...]
    long[rows:, :] = after[...]
    for c in range(rows // CHUNK):
        for p in range(gp.shape[1] // LANES):
            s = lanes_of(p)
            value = jnp.zeros((CHUNK, LANES), f32)
            for k in range(4):
                start = c * CHUNK + 3 - k
                value = value + conv_w[k : k + 1, s] * long[start : start + CHUNK, s]
            low[rows_of(c), s] = value.astype(bf16)
    for r, target in enumerate((own, to1, to2, to3)):
        c = lax.rem(at[0] + r, XS)
        here = pl.ds(pl.multiple_of(c * CHUNK, CHUNK), CHUNK)
        target[...] = (
            dot(dgate[here, :], w_gate[...], NT) + dot(low[here, :], w_mix[...], NT)
        ).astype(bf16)


def shards(tokens, cotangent, decay, in_w, out_w, conv_w, dskip, norm_w):
    tm, stream = lax.axis_size("tm"), lax.axis_size("stream")
    me_t, me_s = lax.axis_index("tm"), lax.axis_index("stream")
    mine = lax.rem(me_t, XS)
    core = lax.rem(me_s, 2)
    heads = dskip.shape[0]
    inner = norm_w.shape[0]
    model = tokens.shape[2]
    state = (in_w.shape[1] - 2 * inner) // 2
    part_heads, width = heads // XS, inner // XS
    rows = XS * tokens.shape[1]
    x_groups = [[h * XS + i for i in range(XS)] for h in range(tm // XS)]
    up = [(i, i + XS) for i in range(XS)]
    down = [(i + XS, i) for i in range(XS)]

    def own(array, axis, size):
        return lax.dynamic_slice_in_dim(array, mine * size, size, axis)

    def along_x(array, steps):
        pairs = [(h * XS + i, h * XS + (i + steps) % XS) for h in range(tm // XS) for i in range(XS)]
        return lax.ppermute(array, "tm", pairs)

    def swap_x(array):
        return lax.all_to_all(array, "tm", 0, 0, axis_index_groups=x_groups)

    cores = [[i for i in range(stream) if i % 2 == c] for c in range(2)]
    half = stream // 2

    def gather_weights(wide):
        same = lax.all_to_all(wide, "stream", 0, 0, axis_index_groups=cores)
        return same, lax.ppermute(same, "stream", [(i, i ^ 1) for i in range(stream)])

    piece = 2 * out_w.shape[0] // XS
    routes = []
    for t in range(tm):
        for s in range(stream):
            group, place = divmod(s, stream // XS)
            target = (t // XS * XS + group, XS * place + t % XS)
            routes.append((t * stream + s, target[0] * stream + target[1]))
    out_piece = lax.ppermute(own(out_w.reshape(-1, width), 0, piece), ("tm", "stream"), routes)
    at = jnp.stack([mine, core]).astype(jnp.int32)
    block = tokens.shape[1]
    short = in_w.shape[0]
    mixed = width + 2 * state
    wide1, gate_w, aux_own, *sends = kernel_call(
        prepare,
        [out((half, short, mixed), bf16), out((short, width), bf16), out((8, model), bf16)]
        + [out((2 * block + 8, model), bf16)] * (XS - 1),
        decay[0].T, in_w, tokens[0], cotangent[0],
        scalars=at, scratch=[pltpu.VMEM((XS, 8, model), f32)],
    )
    recv = []
    for r in range(1, XS):
        recv.append(along_x(sends[r - 1], r))
    same1, other1 = gather_weights(wide1)
    tails = [piece[block - 8 : block] for piece in [tokens[0]] + recv]
    tail = lax.dynamic_index_in_dim(jnp.stack(tails), lax.rem(mine + 1, XS), 0, False)
    halo = lax.ppermute(tail, "tm", up)
    wide2 = jnp.concatenate([gate_w, out_piece], axis=1)
    wide2 = jnp.broadcast_to(wide2[None], (half,) + wide2.shape)
    wide2, same1 = lax.optimization_barrier((wide2, same1))
    same2, other2 = gather_weights(wide2)

    taps = jnp.concatenate([own(conv_w[:, :inner], 1, width), conv_w[:, inner:]], axis=1)
    gain = own(norm_w, 0, width)[None]
    skip = jnp.repeat(own(dskip, 0, part_heads), width // part_heads)[None]
    index = jnp.arange(model)
    source = index // 3 % tm * (3 * stream) + index // (3 * tm) * 3 + index % 3
    perm = (source[:, None] == index[None, :]).astype(bf16)

    chunks = rows // CHUNK
    tok, cot, w_mix, cum, cum_t, pre, conv, states, last = kernel_call(
        project,
        [out((rows, model), bf16), out((rows, model), bf16), out((model, mixed), bf16),
         out((rows, width), f32), out((chunks, 8, CHUNK), f32), out((rows, mixed), f32),
         out((rows, mixed), bf16), out((chunks, state, width), f32), out((state, width), bf16)],
        tokens[0], cotangent[0], aux_own, *recv, halo, same1, other1, taps,
        scalars=at,
        scratch=[pltpu.VMEM((rows + 8, mixed), f32)],
    )
    entering = lax.ppermute(last, "tm", up)
    (y_in,) = kernel_call(inside, [out((rows, width), f32)], conv, cum, cum_t, skip)
    y, full, gate, dn, part, stats, w_gate = kernel_call(
        gated,
        [out((rows, width), f32), out(states.shape, bf16), out((rows, width), bf16),
         out((rows, width), f32), out((XS, block, model), bf16), out((2, rows), f32),
         out((model, width), bf16)],
        conv, cum, states, entering, y_in, tok, cot, same2, other2, gain,
        scalars=at,
        scratch=[pltpu.VMEM((width // LANES, model, LANES), f32), pltpu.VMEM((width, model), bf16)],
    )
    others = []
    for r in range(1, XS):
        others.append(along_x(stats, r))
    parts = swap_x(part)
    factors, dgate, dy, ends, first, dw = kernel_call(
        functools.partial(normed_part, inner),
        [out((chunks, CHUNK, LANES), f32), out((rows, width), bf16), out((rows, width), f32),
         out(states.shape, f32), out((state, width), bf16), out((model, width), bf16)],
        y, gate, dn, stats, *others, conv, cum, gain, cot, perm,
        scratch=[pltpu.VMEM((rows, width), bf16)],
    )
    leaving = lax.ppermute(first, "tm", down)
    dx, dbc, head = kernel_call(
        inside_back,
        [out((rows, width), f32), out((rows, 2 * state), f32), out((8, mixed), f32)],
        conv, cum, cum_t, skip, dy, full, ends, pre,
    )
    after = lax.ppermute(head, "tm", down)
    pieces = lax.all_to_all(dw.reshape(stream, -1, width), "stream", 0, 0)
    gp, result = kernel_call(
        conv_grad,
        [out((rows, mixed), f32), out((block, model), bf16)],
        conv, cum, full, ends, leaving, dy, dx, dbc, pre, parts, factors,
        scalars=at,
    )
    token_parts = kernel_call(
        token_grad,
        [out((block, model), bf16)] * XS,
        gp, after, taps, dgate, w_gate, w_mix,
        scalars=at,
        scratch=[pltpu.VMEM((rows + 8, mixed), f32), pltpu.VMEM((rows, mixed), bf16)],
    )
    moved = []
    for r in range(1, XS):
        moved.append(along_x(token_parts[r], r))
    grad_tokens = sum((p.astype(f32) for p in moved), token_parts[0].astype(f32)).astype(bf16)
    summed = pieces.astype(f32).sum(axis=0).reshape(tm, 3, width)
    swapped = lax.all_to_all(summed, "tm", 0, 0)
    swapped = swapped.reshape(tm // XS, XS, 3, width).sum(axis=0)
    scale = (stream * tm * block) ** (-0.5)
    grad_out_t = jnp.transpose(swapped, (1, 0, 2)).reshape(3, inner) * scale
    return (result[None], grad_tokens[None], grad_out_t)


def solution(mesh):
    data = P("stream", "tm", None)
    in_specs = (data, data, data, P("stream", None), P("stream", None), P(), P(), P())
    out_specs = (data, data, P(("tm", "stream"), None))

    return jax.shard_map(shards, mesh=mesh, in_specs=in_specs, out_specs=out_specs, check_vma=False)
```

```python
import functools

import jax
import jax.numpy as jnp
from jax import lax
from jax.experimental import pallas as pl
from jax.experimental.pallas import tpu as pltpu
from jax.sharding import PartitionSpec as P


bf16, f32 = jnp.bfloat16, jnp.float32
CHUNK = 128
LANES = 128
LIMIT = None
XS = 4
NN = (((1,), (0,)), ((), ()))
NT = (((1,), (1,)), ((), ()))
TN = (((0,), (0,)), ((), ()))


def dot(a, b, dims=NN):
    return lax.dot_general(a.astype(bf16), b.astype(bf16), dims, preferred_element_type=f32)


def exact(a, b, dims=NN):
    return lax.dot_general(
        a, b, dims, precision=lax.Precision.HIGHEST, preferred_element_type=f32
    )


def sig(v):
    return 0.5 + 0.5 * jnp.tanh(0.5 * v)


def kernel_call(body, outs, *args, scalars=None, scratch=(), flops=10**8, limit=None):
    spec = pl.BlockSpec(memory_space=pltpu.VMEM)
    size = sum(a.size * a.dtype.itemsize for a in args) + sum(
        o.size * o.dtype.itemsize for o in outs
    )
    first = [] if scalars is None else [scalars]
    return pl.pallas_call(
        body,
        out_shape=outs,
        in_specs=[pl.BlockSpec(memory_space=pltpu.SMEM)] * len(first) + [spec] * len(args),
        out_specs=[spec] * len(outs),
        scratch_shapes=list(scratch),
        compiler_params=pltpu.CompilerParams(vmem_limit_bytes=limit or LIMIT),
        cost_estimate=pl.CostEstimate(flops=flops, bytes_accessed=size, transcendentals=0),
    )(*first, *args)


def out(shape, dtype):
    return jax.ShapeDtypeStruct(shape, dtype)


def rows_of(c):
    return slice(c * CHUNK, (c + 1) * CHUNK)


def lanes_of(p):
    return slice(p * LANES, (p + 1) * LANES)


def halves():
    return lax.broadcasted_iota(jnp.int32, (CHUNK, LANES), 1) < LANES // 2


def causal():
    later = lax.broadcasted_iota(jnp.int32, (CHUNK, CHUNK), 0)
    return later >= lax.broadcasted_iota(jnp.int32, (CHUNK, CHUNK), 1)


def fades(cum_ref, cum_t_ref, c, head):
    column = cum_ref[rows_of(c), head * 64 : head * 64 + 1]
    row = cum_t_ref[c, head : head + 1, :]
    return jnp.where(causal(), jnp.exp(jnp.minimum(column - row, 0.0)), 0.0)


def place(at, r):
    chunk = lax.rem(at[0] + (XS - r), XS)
    return chunk, pl.ds(pl.multiple_of(chunk * CHUNK, CHUNK), CHUNK)


def prepare(at, in_w, wide, gate_w):
    width = gate_w.shape[1]
    inner = XS * width
    start = pl.multiple_of(at[0] * width, width)
    for i in range(wide.shape[0]):
        wide[i, :, :width] = in_w[:, pl.ds(inner + start, width)]
        wide[i, :, width:] = in_w[:, 2 * inner :]
    gate_w[...] = in_w[:, pl.ds(start, width)]


def pack(at, logs, tokens, halo, aux, send1, send2, send3, decays):
    block = logs.shape[1]
    step = lax.broadcasted_iota(jnp.int32, (block, block), 0)
    upto = (step <= lax.broadcasted_iota(jnp.int32, (block, block), 1)).astype(f32)
    cum = exact(jnp.log(logs[...]), upto)
    high = cum.astype(bf16).astype(f32)
    rest = cum - high
    middle = rest.astype(bf16).astype(f32)
    low = rest - middle
    per = logs.shape[0] // XS
    for j in range(XS):
        for i in range(per):
            h = j * per + i
            rows = [high[h : h + 1], middle[h : h + 1], low[h : h + 1], jnp.zeros((5, block), f32)]
            decays[j, :, i * block : (i + 1) * block] = jnp.concatenate(rows, axis=0)
    tail = halo[...].astype(f32)
    tail = jnp.where(lax.broadcasted_iota(jnp.int32, tail.shape, 0) < 3, 0.0, tail)
    aux[...] = (decays[at[0]] + tail).astype(bf16)
    for r, send in enumerate((send1, send2, send3)):
        send[:block, :] = tokens[...]
        send[block:, :] = (decays[lax.rem(at[0] + r + 1, XS)] + tail).astype(bf16)


def assemble(at, same, other, target, lanes):
    own_first = at[1] == 0
    for i in range(same.shape[0]):
        a, b = same[i, :, lanes], other[i, :, lanes]
        target[48 * i : 48 * i + 24, :] = jnp.where(own_first, a, b).astype(target.dtype)
        target[48 * i + 24 : 48 * i + 48, :] = jnp.where(own_first, b, a).astype(target.dtype)


def project(at, tokens, aux, recv1, recv2, recv3, same, other, conv_w,
            w_mix, cum, cum_t, pre, conv, states, last, mix):
    width = last.shape[1]
    chunks = XS
    block = CHUNK
    assemble(at, same, other, w_mix, slice(None))
    halo = jnp.zeros(aux.shape, f32)
    for r, source in enumerate((None, recv1, recv2, recv3)):
        c, _ = place(at, r)
        t = tokens[...] if r == 0 else source[:block, :]
        extra = (aux[...] if r == 0 else source[block:, :]).astype(f32)
        halo = halo + extra
        mix[pl.ds(pl.multiple_of(8 + c * block, 8), block), :] = (
            dot(t, w_mix[...]).astype(bf16).astype(f32)
        )
        total = extra[0:1] + extra[1:2] + extra[2:3]
        heads = [total[:, i * block : (i + 1) * block] for i in range(width // 64)]
        cum_t[c] = jnp.concatenate(heads + [jnp.zeros((8 - len(heads), block), f32)], axis=0)
    mix[:8, :] = dot(halo, w_mix[...]).astype(bf16).astype(f32)
    left = halves()
    state = jnp.zeros(last.shape, f32)
    for c in range(chunks):
        r = rows_of(c)
        square = jnp.concatenate([cum_t[c], jnp.zeros((block - 8, block), f32)], axis=0).T
        for p in range(width // LANES):
            cum[r, lanes_of(p)] = jnp.where(
                left, square[:, 2 * p : 2 * p + 1], square[:, 2 * p + 1 : 2 * p + 2]
            )
        for p in range(mix.shape[1] // LANES):
            s = lanes_of(p)
            value = jnp.zeros((CHUNK, LANES), f32)
            for k in range(4):
                start = 5 + k + c * CHUNK
                value = value + conv_w[k : k + 1, s] * mix[start : start + CHUNK, s]
            pre[r, s] = value
            conv[r, s] = (value * sig(value)).astype(bf16)
        states[c] = state.astype(bf16)
        end = cum[(c + 1) * CHUNK - 1 : (c + 1) * CHUNK, :]
        faded = jnp.exp(end - cum[r, :]) * conv[r, :width].astype(f32)
        state = jnp.exp(end) * state + dot(conv[r, width : width + 128], faded, TN)
    last[...] = state.astype(bf16)


def inside(conv, cum, cum_t, dskip, y):
    width = y.shape[1]
    left = halves()
    for c in range(y.shape[0] // CHUNK):
        r = rows_of(c)
        b, cv = conv[r, width : width + 128], conv[r, width + 128 : width + 256]
        scores = dot(cv, b, NT)
        for p in range(width // LANES):
            s = lanes_of(p)
            x = conv[r, s].astype(f32)
            weight = jnp.concatenate(
                [fades(cum, cum_t, c, 2 * p) * scores, fades(cum, cum_t, c, 2 * p + 1) * scores],
                axis=1,
            )
            both = jnp.concatenate([jnp.where(left, x, 0.0), jnp.where(left, 0.0, x)], axis=0)
            y[r, s] = dot(weight, both) + dskip[:, s] * x


def gated(at, conv, cum, states, entering, y_in, tok0, tok1, tok2, tok3, cot0, cot1, cot2, cot3,
          same, other, norm_w,
          y, full, gate, dn, part, stats, w_gate, raw, w_out):
    width = y.shape[1]
    chunks = y.shape[0] // CHUNK
    assemble(at, same, other, w_gate, slice(0, width))
    for p in range(width // LANES):
        assemble(at, same, other, raw.at[p], slice(width + p * LANES, width + (p + 1) * LANES))
        for k in range(2):
            lanes = slice(k * width + p * LANES, k * width + (p + 1) * LANES)
            w_out[:, lanes] = raw[p, pl.ds(k, width, stride=2), :].astype(bf16)
    for r, (tok, cot) in enumerate(((tok0, cot0), (tok1, cot1), (tok2, cot2), (tok3, cot3))):
        here = place(at, r)[1]
        gate[here, :] = dot(tok[:CHUNK, :], w_gate[...]).astype(bf16)
        dn[here, :] = dot(cot[...], w_out[...], NT) * norm_w[...]
    carried = entering[...].astype(f32)
    ones = jnp.ones((8, LANES), f32)
    for c in range(chunks):
        r = rows_of(c)
        state = states[c].astype(f32) + carried
        full[c] = state.astype(bf16)
        carried = jnp.exp(cum[(c + 1) * CHUNK - 1 : (c + 1) * CHUNK, :]) * carried
        value = y_in[r, :] + jnp.exp(cum[r, :]) * dot(conv[r, width + 128 : width + 256], state)
        y[r, :] = value
        z = gate[r, :].astype(f32)
        g = value * z * sig(z)
        part[c] = dot(g * norm_w[...], w_out[...]).astype(bf16)
        squares, cross = g * g, g * dn[r, :]
        squares = sum(squares[:, lanes_of(p)] for p in range(width // LANES))
        cross = sum(cross[:, lanes_of(p)] for p in range(width // LANES))
        stats[0:1, r] = exact(ones, squares, NT)[0:1]
        stats[1:2, r] = exact(ones, cross, NT)[0:1]


def normed_part(inner, at, y, gate, dn, stats0, stats1, stats2, stats3, conv, cum, norm_w,
                cot0, cot1, cot2, cot3, perm,
                factors, dgate, dy, ends, first, keep, give, low, cot):
    width = y.shape[1]
    chunks = y.shape[0] // CHUNK
    adjoint = jnp.zeros(first.shape, f32)
    for c in reversed(range(chunks)):
        r = rows_of(c)
        sums = stats0[:, r] + stats1[:, r] + stats2[:, r] + stats3[:, r]
        sums = jnp.concatenate([sums, jnp.zeros((CHUNK - 2, CHUNK), f32)], axis=0).T
        factor = lax.rsqrt(sums[:, 0:1] * (1.0 / inner) + 1e-05)
        lean = factor * factor * sums[:, 1:2] * (1.0 / inner)
        factors[c] = jnp.broadcast_to(factor, (CHUNK, LANES))
        z = gate[r, :].astype(f32)
        q = sig(z)
        value = y[r, :]
        g = value * z * q
        low[r, :] = (g * factor * norm_w[...]).astype(bf16)
        dg = factor * (dn[r, :] - g * lean)
        dvalue = dg * z * q
        dy[r, :] = dvalue
        dgate[r, :] = (dg * value * q * (1.0 + z * (1.0 - q))).astype(bf16)
        ends[c] = adjoint
        end = cum[(c + 1) * CHUNK - 1 : (c + 1) * CHUNK, :]
        adjoint = jnp.exp(end) * adjoint + dot(
            conv[r, width + 128 : width + 256], jnp.exp(cum[r, :]) * dvalue, TN
        )
    first[...] = adjoint.astype(bf16)
    for r, source in enumerate((cot0, cot1, cot2, cot3)):
        cot[place(at, r)[1], :] = source[...]
    summed = dot(cot[...], low[...], TN)
    keep[...] = dot(perm[: keep.shape[0], :], summed).astype(bf16)
    give[...] = dot(perm[keep.shape[0] :, :], summed).astype(bf16)


def inside_back(conv, cum, cum_t, dskip, dy, full, ends, pre, keep, got, dx, dbc, head, pair):
    pair[...] = (keep[...].astype(f32) + got[...].astype(f32)).astype(bf16)
    width = dy.shape[1]
    left = halves()
    for c in range(dy.shape[0] // CHUNK):
        r = rows_of(c)
        b, cv = conv[r, width : width + 128], conv[r, width + 128 : width + 256]
        scores = dot(cv, b, NT)
        dscores = jnp.zeros((CHUNK, CHUNK), f32)
        for p in range(width // LANES):
            s = lanes_of(p)
            x = conv[r, s]
            d = dy[r, s]
            da, db = jnp.where(left, d, 0.0), jnp.where(left, 0.0, d)
            fa, fb = fades(cum, cum_t, c, 2 * p), fades(cum, cum_t, c, 2 * p + 1)
            weight = jnp.concatenate([fa * scores, fb * scores], axis=0)
            dx[r, s] = dot(weight, jnp.concatenate([da, db], axis=0), TN) + dskip[:, s] * d
            dscores = dscores + fa * dot(da, x, NT) + fb * dot(db, x, NT)
        dbc[r, :128] = dot(dscores, cv, TN)
        dbc[r, 128:] = dot(dscores, b)
    first = conv_rows(conv, cum, full[0], ends[0], dy, dx, dbc, pre, 0, 16)
    for lanes, value in first:
        head[:, lanes] = value[:8]


def conv_rows(conv, cum, state, adjoint, dy, dx, dbc, pre, start, count):
    width = dy.shape[1]
    r = slice(start, start + count)
    chunk_end = start // CHUNK * CHUNK + CHUNK
    fade = jnp.exp(cum[chunk_end - 1 : chunk_end, :] - cum[r, :])
    grad_x = dx[r, :] + fade * dot(conv[r, width : width + 128], adjoint)
    grad_b = dbc[r, :128] + dot(fade * conv[r, :width].astype(f32), adjoint, NT)
    grad_c = dbc[r, 128:] + dot(jnp.exp(cum[r, :]) * dy[r, :], state, NT)
    result = []
    for lanes, grad in (
        (slice(0, width), grad_x),
        (slice(width, width + 128), grad_b),
        (slice(width + 128, width + 256), grad_c),
    ):
        v = pre[r, lanes]
        q = sig(v)
        result.append((lanes, grad * q * (1.0 + v * (1.0 - q))))
    return result


def conv_grad(at, conv, cum, full, ends, leaving, dy, dx, dbc, pre, parts, factors, gp, result):
    chunks = dy.shape[0] // CHUNK
    carried = leaving[...].astype(f32)
    for c in reversed(range(chunks)):
        adjoint = ends[c] + carried
        end = cum[(c + 1) * CHUNK - 1 : (c + 1) * CHUNK, :]
        carried = jnp.exp(end) * carried
        rows = conv_rows(conv, cum, full[c], adjoint, dy, dx, dbc, pre, c * CHUNK, CHUNK)
        for lanes, value in rows:
            gp[rows_of(c), lanes] = value
    factor = factors[at[0]]
    for p in range(result.shape[1] // LANES):
        s = lanes_of(p)
        total = sum(parts[k, :, s].astype(f32) for k in range(XS))
        result[:, s] = (total * factor).astype(bf16)


def token_grad(at, gp, after, conv_w, dgate, w_gate, w_mix, own, to1, to2, to3, long, low):
    rows = gp.shape[0]
    long[:rows, :] = gp[...]
    long[rows:, :] = after[...]
    for c in range(rows // CHUNK):
        for p in range(gp.shape[1] // LANES):
            s = lanes_of(p)
            value = jnp.zeros((CHUNK, LANES), f32)
            for k in range(4):
                start = c * CHUNK + 3 - k
                value = value + conv_w[k : k + 1, s] * long[start : start + CHUNK, s]
            low[rows_of(c), s] = value.astype(bf16)
    for r, target in enumerate((own, to1, to2, to3)):
        c = lax.rem(at[0] + r, XS)
        here = pl.ds(pl.multiple_of(c * CHUNK, CHUNK), CHUNK)
        target[...] = (
            dot(dgate[here, :], w_gate[...], NT) + dot(low[here, :], w_mix[...], NT)
        ).astype(bf16)


def shards(tokens, cotangent, decay, in_w, out_w, conv_w, dskip, norm_w):
    tm, stream = lax.axis_size("tm"), lax.axis_size("stream")
    me_t, me_s = lax.axis_index("tm"), lax.axis_index("stream")
    mine = lax.rem(me_t, XS)
    core = lax.rem(me_s, 2)
    heads = dskip.shape[0]
    inner = norm_w.shape[0]
    model = tokens.shape[2]
    state = (in_w.shape[1] - 2 * inner) // 2
    part_heads, width = heads // XS, inner // XS
    rows = XS * tokens.shape[1]
    x_groups = [[h * XS + i for i in range(XS)] for h in range(tm // XS)]
    up = [(i, i + XS) for i in range(XS)]
    down = [(i + XS, i) for i in range(XS)]

    def own(array, axis, size):
        return lax.dynamic_slice_in_dim(array, mine * size, size, axis)

    def along_x(array, steps):
        pairs = [(h * XS + i, h * XS + (i + steps) % XS) for h in range(tm // XS) for i in range(XS)]
        return lax.ppermute(array, "tm", pairs)

    def swap_x(array):
        return lax.all_to_all(array, "tm", 0, 0, axis_index_groups=x_groups)

    cores = [[i for i in range(stream) if i % 2 == c] for c in range(2)]
    half = stream // 2

    def gather_weights(wide):
        same = lax.all_to_all(wide, "stream", 0, 0, axis_index_groups=cores)
        return same, lax.ppermute(same, "stream", [(i, i ^ 1) for i in range(stream)])

    halo = lax.ppermute(tokens[0, -8:], "tm", [(XS - 1, XS)])
    at = jnp.stack([mine, core]).astype(jnp.int32)
    block = tokens.shape[1]
    short = in_w.shape[0]
    mixed = width + 2 * state
    wide1, gate_w = kernel_call(
        prepare,
        [out((half, short, mixed), bf16), out((short, width), bf16)],
        in_w, scalars=at,
    )
    same1, other1 = gather_weights(wide1)
    aux, *sends = kernel_call(
        pack,
        [out((8, model), bf16)] + [out((block + 8, model), bf16)] * (XS - 1),
        decay[0].T, tokens[0], halo,
        scalars=at, scratch=[pltpu.VMEM((XS, 8, model), f32)],
    )
    toks, cots = [tokens[0]], [cotangent[0]]
    for r in range(1, XS):
        toks.append(along_x(sends[r - 1], r))
        cots.append(along_x(cotangent[0], r))
    piece = 2 * out_w.shape[0] // XS
    routes = []
    for t in range(tm):
        for s in range(stream):
            group, place_ = divmod(s, stream // XS)
            target = (t // XS * XS + group, XS * place_ + t % XS)
            routes.append((t * stream + s, target[0] * stream + target[1]))
    out_piece = lax.ppermute(own(out_w.reshape(-1, width), 0, piece), ("tm", "stream"), routes)
    wide2 = jnp.concatenate([gate_w, out_piece], axis=1)
    wide2 = jnp.broadcast_to(wide2[None], (half,) + wide2.shape)
    same2, other2 = gather_weights(wide2)

    taps = jnp.concatenate([own(conv_w[:, :inner], 1, width), conv_w[:, inner:]], axis=1)
    gain = own(norm_w, 0, width)[None]
    skip = jnp.repeat(own(dskip, 0, part_heads), width // part_heads)[None]
    index = jnp.arange(model)
    late, spot = index // (model // 2), index % (model // 2)
    target = 2 * (spot // (3 * tm)) + jnp.where(late == 0, core, 1 - core)
    source = index // 3 % tm * (3 * stream) + target * 3 + index % 3
    perm = (source[:, None] == index[None, :]).astype(bf16)

    chunks = rows // CHUNK
    w_mix, cum, cum_t, pre, conv, states, last = kernel_call(
        project,
        [out((model, mixed), bf16), out((rows, width), f32), out((chunks, 8, CHUNK), f32),
         out((rows, mixed), f32), out((rows, mixed), bf16), out((chunks, state, width), bf16),
         out((state, width), bf16)],
        tokens[0], aux, *toks[1:], same1, other1, taps,
        scalars=at,
        scratch=[pltpu.VMEM((rows + 8, mixed), f32)],
    )
    entering = lax.ppermute(last, "tm", up)
    (y_in,) = kernel_call(inside, [out((rows, width), f32)], conv, cum, cum_t, skip)
    y, full, gate, dn, part, stats, w_gate = kernel_call(
        gated,
        [out((rows, width), f32), out(states.shape, bf16), out((rows, width), bf16),
         out((rows, width), f32), out((XS, block, model), bf16), out((2, rows), f32),
         out((model, width), bf16)],
        conv, cum, states, entering, y_in, *toks, *cots, same2, other2, gain,
        scalars=at,
        scratch=[pltpu.VMEM((width // LANES, model, LANES), f32), pltpu.VMEM((width, model), bf16)],
    )
    others = []
    for r in range(1, XS):
        others.append(along_x(stats, r))
    parts = swap_x(part)
    factors, dgate, dy, ends, first, keep, give = kernel_call(
        functools.partial(normed_part, inner),
        [out((chunks, CHUNK, LANES), f32), out((rows, width), bf16), out((rows, width), f32),
         out(states.shape, f32), out((state, width), bf16), out((model // 2, width), bf16),
         out((model // 2, width), bf16)],
        y, gate, dn, stats, *others, conv, cum, gain, *cots, perm,
        scalars=at,
        scratch=[pltpu.VMEM((rows, width), bf16), pltpu.VMEM((rows, model), bf16)],
    )
    leaving = lax.ppermute(first, "tm", down)
    got = lax.ppermute(give, "stream", [(i, i ^ 1) for i in range(stream)])
    dx, dbc, head, pair = kernel_call(
        inside_back,
        [out((rows, width), f32), out((rows, 2 * state), f32), out((8, mixed), f32),
         out(keep.shape, bf16)],
        conv, cum, cum_t, skip, dy, full, ends, pre, keep, got,
    )
    after = lax.ppermute(head, "tm", down)
    pieces = lax.all_to_all(pair.reshape(half, -1, width), "stream", 0, 0, axis_index_groups=cores)
    gp, result = kernel_call(
        conv_grad,
        [out((rows, mixed), f32), out((block, model), bf16)],
        conv, cum, full, ends, leaving, dy, dx, dbc, pre, parts, factors,
        scalars=at,
    )
    token_parts = kernel_call(
        token_grad,
        [out((block, model), bf16)] * XS,
        gp, after, taps, dgate, w_gate, w_mix,
        scalars=at,
        scratch=[pltpu.VMEM((rows + 8, mixed), f32), pltpu.VMEM((rows, mixed), bf16)],
    )
    moved = []
    for r in range(1, XS):
        moved.append(along_x(token_parts[r], r))
    grad_tokens = sum((p.astype(f32) for p in moved), token_parts[0].astype(f32)).astype(bf16)
    summed = pieces.astype(f32).sum(axis=0).reshape(tm, 3, width)
    swapped = lax.all_to_all(summed, "tm", 0, 0)
    swapped = swapped.reshape(tm // XS, XS, 3, width).sum(axis=0)
    scale = (stream * tm * block) ** (-0.5)
    grad_out_t = jnp.transpose(swapped, (1, 0, 2)).reshape(3, inner) * scale
    return (result[None], grad_tokens[None], grad_out_t)


def solution(mesh):
    data = P("stream", "tm", None)
    in_specs = (data, data, data, P("stream", None), P("stream", None), P(), P(), P())
    out_specs = (data, data, P(("tm", "stream"), None))

    return jax.shard_map(shards, mesh=mesh, in_specs=in_specs, out_specs=out_specs, check_vma=False)
```

```python
import functools

import jax
import jax.numpy as jnp
from jax import lax
from jax.experimental import pallas as pl
from jax.experimental.pallas import tpu as pltpu
from jax.sharding import PartitionSpec as P


bf16, f32 = jnp.bfloat16, jnp.float32
CHUNK = 128
LANES = 128
LIMIT = None
XS = 4
NN = (((1,), (0,)), ((), ()))
NT = (((1,), (1,)), ((), ()))
TN = (((0,), (0,)), ((), ()))


def dot(a, b, dims=NN):
    return lax.dot_general(a.astype(bf16), b.astype(bf16), dims, preferred_element_type=f32)


def exact(a, b, dims=NN):
    return lax.dot_general(
        a, b, dims, precision=lax.Precision.HIGHEST, preferred_element_type=f32
    )


def sig(v):
    return 0.5 + 0.5 * jnp.tanh(0.5 * v)


def kernel_call(body, outs, *args, scalars=None, scratch=(), flops=10**8):
    spec = pl.BlockSpec(memory_space=pltpu.VMEM)
    size = sum(a.size * a.dtype.itemsize for a in list(args) + list(outs))
    first = [] if scalars is None else [scalars]
    return pl.pallas_call(
        body,
        out_shape=outs,
        in_specs=[pl.BlockSpec(memory_space=pltpu.SMEM)] * len(first) + [spec] * len(args),
        out_specs=[spec] * len(outs),
        scratch_shapes=list(scratch),
        compiler_params=pltpu.CompilerParams(vmem_limit_bytes=LIMIT),
        cost_estimate=pl.CostEstimate(flops=flops, bytes_accessed=size, transcendentals=0),
    )(*first, *args)


def out(shape, dtype):
    return jax.ShapeDtypeStruct(shape, dtype)


def rows_of(c):
    return slice(c * CHUNK, (c + 1) * CHUNK)


def lanes_of(p):
    return slice(p * LANES, (p + 1) * LANES)


def halves():
    return lax.broadcasted_iota(jnp.int32, (CHUNK, LANES), 1) < LANES // 2


def causal():
    later = lax.broadcasted_iota(jnp.int32, (CHUNK, CHUNK), 0)
    return later >= lax.broadcasted_iota(jnp.int32, (CHUNK, CHUNK), 1)


def fades(cum_ref, cum_t_ref, c, head):
    column = cum_ref[rows_of(c), head * 64 : head * 64 + 1]
    row = cum_t_ref[c, head : head + 1, :]
    return jnp.where(causal(), jnp.exp(jnp.minimum(column - row, 0.0)), 0.0)


def place(at, r):
    chunk = lax.rem(at[0] + (XS - r), XS)
    return chunk, pl.ds(pl.multiple_of(chunk * CHUNK, CHUNK), CHUNK)


def prepare(at, in_w, wide, gate_w):
    width = gate_w.shape[1]
    inner = XS * width
    start = pl.multiple_of(at[0] * width, width)
    for i in range(wide.shape[0]):
        wide[i, :, :width] = in_w[:, pl.ds(inner + start, width)]
        wide[i, :, width:] = in_w[:, 2 * inner :]
    gate_w[...] = in_w[:, pl.ds(start, width)]


def pack(at, logs, tokens, cotangent, halo, aux, send1, send2, send3, decays):
    block = logs.shape[1]
    step = lax.broadcasted_iota(jnp.int32, (block, block), 0)
    upto = (step <= lax.broadcasted_iota(jnp.int32, (block, block), 1)).astype(f32)
    cum = exact(jnp.log(logs[...]), upto)
    high = cum.astype(bf16).astype(f32)
    rest = cum - high
    middle = rest.astype(bf16).astype(f32)
    low = rest - middle
    per = logs.shape[0] // XS
    for j in range(XS):
        for i in range(per):
            h = j * per + i
            rows = [high[h : h + 1], middle[h : h + 1], low[h : h + 1], jnp.zeros((5, block), f32)]
            decays[j, :, i * block : (i + 1) * block] = jnp.concatenate(rows, axis=0)
    tail = halo[...].astype(f32)
    tail = jnp.where(lax.broadcasted_iota(jnp.int32, tail.shape, 0) < 3, 0.0, tail)
    aux[...] = (decays[at[0]] + tail).astype(bf16)
    for r, send in enumerate((send1, send2, send3)):
        send[:block, :] = tokens[...]
        send[block : 2 * block, :] = cotangent[...]
        send[2 * block :, :] = (decays[lax.rem(at[0] + r + 1, XS)] + tail).astype(bf16)


def assemble(at, same, other, target, lanes):
    own_first = at[1] == 0
    for i in range(same.shape[0]):
        a, b = same[i, :, lanes], other[i, :, lanes]
        target[48 * i : 48 * i + 24, :] = jnp.where(own_first, a, b).astype(target.dtype)
        target[48 * i + 24 : 48 * i + 48, :] = jnp.where(own_first, b, a).astype(target.dtype)


def project(at, tokens, aux, recv1, recv2, recv3, same, other, conv_w,
            w_mix, cum, cum_t, pre, conv, states, last, mix):
    width = last.shape[1]
    chunks = XS
    block = CHUNK
    assemble(at, same, other, w_mix, slice(None))
    halo = jnp.zeros(aux.shape, f32)
    for r, source in enumerate((None, recv1, recv2, recv3)):
        c, _ = place(at, r)
        t = tokens[...] if r == 0 else source[:block, :]
        extra = (aux[...] if r == 0 else source[2 * block :, :]).astype(f32)
        halo = halo + extra
        mix[pl.ds(pl.multiple_of(8 + c * block, 8), block), :] = (
            dot(t, w_mix[...]).astype(bf16).astype(f32)
        )
        total = extra[0:1] + extra[1:2] + extra[2:3]
        heads = [total[:, i * block : (i + 1) * block] for i in range(width // 64)]
        cum_t[c] = jnp.concatenate(heads + [jnp.zeros((8 - len(heads), block), f32)], axis=0)
    mix[:8, :] = dot(halo, w_mix[...]).astype(bf16).astype(f32)
    left = halves()
    state = jnp.zeros(last.shape, f32)
    for c in range(chunks):
        r = rows_of(c)
        square = jnp.concatenate([cum_t[c], jnp.zeros((block - 8, block), f32)], axis=0).T
        for p in range(width // LANES):
            cum[r, lanes_of(p)] = jnp.where(
                left, square[:, 2 * p : 2 * p + 1], square[:, 2 * p + 1 : 2 * p + 2]
            )
        for p in range(mix.shape[1] // LANES):
            s = lanes_of(p)
            value = jnp.zeros((CHUNK, LANES), f32)
            for k in range(4):
                start = 5 + k + c * CHUNK
                value = value + conv_w[k : k + 1, s] * mix[start : start + CHUNK, s]
            pre[r, s] = value.astype(bf16)
            conv[r, s] = (value * sig(value)).astype(bf16)
        states[c] = state.astype(bf16)
        end = cum[(c + 1) * CHUNK - 1 : (c + 1) * CHUNK, :]
        faded = jnp.exp(end - cum[r, :]) * conv[r, :width].astype(f32)
        state = jnp.exp(end) * state + dot(conv[r, width : width + 128], faded, TN)
    last[...] = state.astype(bf16)


def inside(conv, cum, cum_t, dskip, y):
    width = y.shape[1]
    left = halves()
    for c in range(y.shape[0] // CHUNK):
        r = rows_of(c)
        b, cv = conv[r, width : width + 128], conv[r, width + 128 : width + 256]
        scores = dot(cv, b, NT)
        for p in range(width // LANES):
            s = lanes_of(p)
            x = conv[r, s].astype(f32)
            weight = jnp.concatenate(
                [fades(cum, cum_t, c, 2 * p) * scores, fades(cum, cum_t, c, 2 * p + 1) * scores],
                axis=1,
            )
            both = jnp.concatenate([jnp.where(left, x, 0.0), jnp.where(left, 0.0, x)], axis=0)
            y[r, s] = (dot(weight, both) + dskip[:, s] * x).astype(y.dtype)


def gated(at, conv, cum, states, entering, y_in, tok0, cot0, tok1, tok2, tok3, same, other, norm_w,
          y, full, gate, dn, part, stats, w_gate, raw, w_out):
    width = y.shape[1]
    chunks = y.shape[0] // CHUNK
    assemble(at, same, other, w_gate, slice(0, width))
    for p in range(width // LANES):
        assemble(at, same, other, raw.at[p], slice(width + p * LANES, width + (p + 1) * LANES))
        for k in range(2):
            lanes = slice(k * width + p * LANES, k * width + (p + 1) * LANES)
            w_out[:, lanes] = raw[p, pl.ds(k, width, stride=2), :].astype(bf16)
    for r, tok in enumerate((tok0, tok1, tok2, tok3)):
        here = place(at, r)[1]
        gate[here, :] = dot(tok[:CHUNK, :], w_gate[...]).astype(bf16)
        cot = cot0[...] if r == 0 else tok[CHUNK : 2 * CHUNK, :]
        dn[here, :] = (dot(cot, w_out[...], NT) * norm_w[...]).astype(dn.dtype)
    carried = entering[...].astype(f32)
    ones = jnp.ones((8, LANES), f32)
    for c in range(chunks):
        r = rows_of(c)
        state = states[c].astype(f32) + carried
        full[c] = state.astype(bf16)
        carried = jnp.exp(cum[(c + 1) * CHUNK - 1 : (c + 1) * CHUNK, :]) * carried
        value = y_in[r, :].astype(f32) + jnp.exp(cum[r, :]) * dot(conv[r, width + 128 : width + 256], state)
        y[r, :] = value
        z = gate[r, :].astype(f32)
        g = value * z * sig(z)
        part[c] = dot(g * norm_w[...], w_out[...]).astype(bf16)
        squares, cross = g * g, g * dn[r, :].astype(f32)
        squares = sum(squares[:, lanes_of(p)] for p in range(width // LANES))
        cross = sum(cross[:, lanes_of(p)] for p in range(width // LANES))
        stats[0:1, r] = exact(ones, squares, NT)[0:1]
        stats[1:2, r] = exact(ones, cross, NT)[0:1]


def normed_part(inner, at, y, gate, dn, stats0, stats1, stats2, stats3, conv, cum, norm_w,
                cot0, cot1, cot2, cot3, perm,
                factors, dgate, dy, ends, first, keep, give, low, cot):
    width = y.shape[1]
    chunks = y.shape[0] // CHUNK
    adjoint = jnp.zeros(first.shape, f32)
    for c in reversed(range(chunks)):
        r = rows_of(c)
        sums = stats0[:, r] + stats1[:, r] + stats2[:, r] + stats3[:, r]
        sums = jnp.concatenate([sums, jnp.zeros((CHUNK - 2, CHUNK), f32)], axis=0).T
        factor = lax.rsqrt(sums[:, 0:1] * (1.0 / inner) + 1e-05)
        lean = factor * factor * sums[:, 1:2] * (1.0 / inner)
        factors[c] = jnp.broadcast_to(factor, (CHUNK, LANES))
        z = gate[r, :].astype(f32)
        q = sig(z)
        value = y[r, :]
        g = value * z * q
        low[r, :] = (g * factor * norm_w[...]).astype(bf16)
        dg = factor * (dn[r, :].astype(f32) - g * lean)
        dvalue = dg * z * q
        dy[r, :] = dvalue.astype(bf16)
        dgate[r, :] = (dg * value * q * (1.0 + z * (1.0 - q))).astype(bf16)
        ends[c] = adjoint.astype(bf16)
        end = cum[(c + 1) * CHUNK - 1 : (c + 1) * CHUNK, :]
        adjoint = jnp.exp(end) * adjoint + dot(
            conv[r, width + 128 : width + 256], jnp.exp(cum[r, :]) * dvalue, TN
        )
    first[...] = adjoint.astype(bf16)
    for r, source in enumerate((cot0, cot1, cot2, cot3)):
        cot[place(at, r)[1], :] = source[...] if r == 0 else source[CHUNK : 2 * CHUNK, :]
    summed = dot(cot[...], low[...], TN)
    give[...] = dot(perm[keep.shape[0] :, :], summed).astype(bf16)
    keep[...] = dot(perm[: keep.shape[0], :], summed).astype(bf16)


def inside_back(conv, cum, cum_t, dskip, dy, full, ends, pre, dx, dbc, head):
    width = dy.shape[1]
    left = halves()
    for c in range(dy.shape[0] // CHUNK):
        r = rows_of(c)
        b, cv = conv[r, width : width + 128], conv[r, width + 128 : width + 256]
        scores = dot(cv, b, NT)
        dscores = jnp.zeros((CHUNK, CHUNK), f32)
        for p in range(width // LANES):
            s = lanes_of(p)
            x = conv[r, s]
            d = dy[r, s].astype(f32)
            da, db = jnp.where(left, d, 0.0), jnp.where(left, 0.0, d)
            fa, fb = fades(cum, cum_t, c, 2 * p), fades(cum, cum_t, c, 2 * p + 1)
            weight = jnp.concatenate([fa * scores, fb * scores], axis=0)
            dx[r, s] = (
                dot(weight, jnp.concatenate([da, db], axis=0), TN) + dskip[:, s] * d
            ).astype(dx.dtype)
            dscores = dscores + fa * dot(da, x, NT) + fb * dot(db, x, NT)
        dbc[r, :128] = dot(dscores, cv, TN).astype(dbc.dtype)
        dbc[r, 128:] = dot(dscores, b).astype(dbc.dtype)
    first = conv_rows(conv, cum, full[0], ends[0], dy, dx, dbc, pre, 0, 16)
    for lanes, value in first:
        head[:, lanes] = value[:8]


def conv_rows(conv, cum, state, adjoint, dy, dx, dbc, pre, start, count):
    width = dy.shape[1]
    r = slice(start, start + count)
    chunk_end = start // CHUNK * CHUNK + CHUNK
    fade = jnp.exp(cum[chunk_end - 1 : chunk_end, :] - cum[r, :])
    grad_x = dx[r, :] + fade * dot(conv[r, width : width + 128], adjoint)
    grad_b = dbc[r, :128] + dot(fade * conv[r, :width].astype(f32), adjoint, NT)
    grad_c = dbc[r, 128:] + dot(jnp.exp(cum[r, :]) * dy[r, :].astype(f32), state, NT)
    result = []
    for lanes, grad in (
        (slice(0, width), grad_x),
        (slice(width, width + 128), grad_b),
        (slice(width + 128, width + 256), grad_c),
    ):
        v = pre[r, lanes].astype(f32)
        q = sig(v)
        result.append((lanes, grad * q * (1.0 + v * (1.0 - q))))
    return result


def conv_grad(at, conv, cum, full, ends, leaving, dy, dx, dbc, pre, parts, factors, gp, result):
    chunks = dy.shape[0] // CHUNK
    carried = leaving[...].astype(f32)
    for c in reversed(range(chunks)):
        adjoint = ends[c].astype(f32) + carried
        end = cum[(c + 1) * CHUNK - 1 : (c + 1) * CHUNK, :]
        carried = jnp.exp(end) * carried
        rows = conv_rows(conv, cum, full[c], adjoint, dy, dx, dbc, pre, c * CHUNK, CHUNK)
        for lanes, value in rows:
            gp[rows_of(c), lanes] = value.astype(gp.dtype)
    factor = factors[at[0]]
    for p in range(result.shape[1] // LANES):
        s = lanes_of(p)
        total = sum(parts[k, :, s].astype(f32) for k in range(XS))
        result[:, s] = (total * factor).astype(bf16)


def token_grad(at, gp, after, conv_w, dgate, w_gate, w_mix, pieces,
               own, to1, to2, to3, own_dw, long, low, dws):
    rows = gp.shape[0]
    long[rows:, :] = after[...]
    for c in reversed(range(rows // CHUNK)):
        long[rows_of(c), :] = gp[rows_of(c), :].astype(f32)
        for p in range(gp.shape[1] // LANES):
            s = lanes_of(p)
            value = jnp.zeros((CHUNK, LANES), f32)
            for k in range(4):
                start = c * CHUNK + 3 - k
                value = value + conv_w[k : k + 1, s] * long[start : start + CHUNK, s]
            low[rows_of(c), s] = value.astype(bf16)
    total = sum(pieces[i].astype(f32) for i in range(pieces.shape[0]))
    width = total.shape[1]
    dws[...] = jnp.zeros(dws.shape, f32)
    for x in range(XS):
        dws[x, 0:3, :width] = total[3 * x : 3 * x + 3]
    own_dw[...] = dws[at[0], :, :width]
    for r, target in ((2, to2), (1, to1), (3, to3), (0, own)):
        c = lax.rem(at[0] + r, XS)
        here = pl.ds(pl.multiple_of(c * CHUNK, CHUNK), CHUNK)
        target[:CHUNK, :] = (
            dot(dgate[here, :], w_gate[...], NT) + dot(low[here, :], w_mix[...], NT)
        ).astype(bf16)
        if r:
            target[CHUNK:, :] = dws[c].astype(bf16)


def finish(scale, at, own, own_dw, got1, got2, got3, tokens, dw):
    width = own_dw.shape[1]
    for r, got in enumerate((own_dw, got1, got2, got3)):
        lanes = pl.ds(pl.multiple_of(place(at, r)[0] * width, width), width)
        rows = got[...] if r == 0 else got[CHUNK:, :width].astype(f32)
        dw[:, lanes] = rows[0:3] * scale
    for p in range(tokens.shape[1] // LANES):
        s = lanes_of(p)
        value = own[:, s].astype(f32)
        for got in (got1, got2, got3):
            value = value + got[:CHUNK, s].astype(f32)
        tokens[:, s] = value.astype(bf16)


def shards(tokens, cotangent, decay, in_w, out_w, conv_w, dskip, norm_w):
    tm, stream = lax.axis_size("tm"), lax.axis_size("stream")
    me_t, me_s = lax.axis_index("tm"), lax.axis_index("stream")
    mine = lax.rem(me_t, XS)
    core = lax.rem(me_s, 2)
    heads = dskip.shape[0]
    inner = norm_w.shape[0]
    model = tokens.shape[2]
    state = (in_w.shape[1] - 2 * inner) // 2
    part_heads, width = heads // XS, inner // XS
    rows = XS * tokens.shape[1]
    x_groups = [[h * XS + i for i in range(XS)] for h in range(tm // XS)]
    up = [(i, i + XS) for i in range(XS)]
    down = [(i + XS, i) for i in range(XS)]

    def own(array, axis, size):
        return lax.dynamic_slice_in_dim(array, mine * size, size, axis)

    def along_x(array, steps):
        pairs = [(h * XS + i, h * XS + (i + steps) % XS) for h in range(tm // XS) for i in range(XS)]
        return lax.ppermute(array, "tm", pairs)

    def swap_x(array):
        return lax.all_to_all(array, "tm", 0, 0, axis_index_groups=x_groups)

    cores = [[i for i in range(stream) if i % 2 == c] for c in range(2)]
    half = stream // 2

    def gather_weights(wide):
        same = lax.all_to_all(wide, "stream", 0, 0, axis_index_groups=cores)
        return same, lax.ppermute(same, "stream", [(i, i ^ 1) for i in range(stream)])

    halo = lax.ppermute(tokens[0, -8:], "tm", [(XS - 1, XS)])
    at = jnp.stack([mine, core]).astype(jnp.int32)
    block = tokens.shape[1]
    short = in_w.shape[0]
    mixed = width + 2 * state
    wide1, gate_w = kernel_call(
        prepare,
        [out((half, short, mixed), bf16), out((short, width), bf16)],
        in_w, scalars=at,
    )
    same1, other1 = gather_weights(wide1)
    aux, *sends = kernel_call(
        pack,
        [out((8, model), bf16)] + [out((2 * block + 8, model), bf16)] * (XS - 1),
        decay[0].T, tokens[0], cotangent[0], halo,
        scalars=at, scratch=[pltpu.VMEM((XS, 8, model), f32)],
    )
    recv = []
    for r in range(1, XS):
        recv.append(along_x(sends[r - 1], r))
    piece = 2 * out_w.shape[0] // XS
    routes = []
    for t in range(tm):
        for s in range(stream):
            group, place_ = divmod(s, stream // XS)
            target = (t // XS * XS + group, XS * place_ + t % XS)
            routes.append((t * stream + s, target[0] * stream + target[1]))
    out_piece = lax.ppermute(own(out_w.reshape(-1, width), 0, piece), ("tm", "stream"), routes)
    wide2 = jnp.concatenate([gate_w, out_piece], axis=1)
    wide2 = jnp.broadcast_to(wide2[None], (half,) + wide2.shape)
    same2, other2 = gather_weights(wide2)

    taps = jnp.concatenate([own(conv_w[:, :inner], 1, width), conv_w[:, inner:]], axis=1)
    gain = own(norm_w, 0, width)[None]
    skip = jnp.repeat(own(dskip, 0, part_heads), width // part_heads)[None]
    index = jnp.arange(model)
    quarter = model // 4
    late, far = index // (2 * quarter), index // quarter % 2
    target = 2 * (index % quarter // (3 * XS)) + jnp.where(late == 0, core, 1 - core)
    side = me_t // XS
    target_t = index // 3 % XS + XS * jnp.where(far == 0, side, 1 - side)
    source = target_t * (3 * stream) + target * 3 + index % 3
    perm = (source[:, None] == index[None, :]).astype(bf16)

    chunks = rows // CHUNK
    w_mix, cum, cum_t, pre, conv, states, last = kernel_call(
        project,
        [out((model, mixed), bf16), out((rows, width), f32), out((chunks, 8, CHUNK), f32),
         out((rows, mixed), bf16), out((rows, mixed), bf16), out((chunks, state, width), bf16),
         out((state, width), bf16)],
        tokens[0], aux, *recv, same1, other1, taps,
        scalars=at,
        scratch=[pltpu.VMEM((rows + 8, mixed), f32)],
    )
    entering = lax.ppermute(last, "tm", up)
    (y_in,) = kernel_call(inside, [out((rows, width), f32)], conv, cum, cum_t, skip)
    y, full, gate, dn, part, stats, w_gate = kernel_call(
        gated,
        [out((rows, width), f32), out(states.shape, bf16), out((rows, width), bf16),
         out((rows, width), bf16), out((XS, block, model), bf16), out((2, rows), f32),
         out((model, width), bf16)],
        conv, cum, states, entering, y_in, tokens[0], cotangent[0], *recv, same2, other2, gain,
        scalars=at,
        scratch=[pltpu.VMEM((width // LANES, model, LANES), f32), pltpu.VMEM((width, model), bf16)],
    )
    others = []
    for r in range(1, XS):
        others.append(along_x(stats, r))
    parts = swap_x(part)
    factors, dgate, dy, ends, first, keep, give = kernel_call(
        functools.partial(normed_part, inner),
        [out((chunks, CHUNK, LANES), f32), out((rows, width), bf16), out((rows, width), bf16),
         out(states.shape, bf16), out((state, width), bf16), out((model // 2, width), bf16),
         out((model // 2, width), bf16)],
        y, gate, dn, stats, *others, conv, cum, gain, cotangent[0], *recv, perm,
        scalars=at,
        scratch=[pltpu.VMEM((rows, width), bf16), pltpu.VMEM((rows, model), bf16)],
    )
    leaving = lax.ppermute(first, "tm", down)
    got = lax.ppermute(give, "stream", [(i, i ^ 1) for i in range(stream)])
    pair = keep.astype(f32) + got.astype(f32)
    swap = [(i, (i + XS) % tm) for i in range(tm)]
    crossed = lax.ppermute(pair[quarter:].astype(bf16), "tm", swap)
    dx, dbc, head = kernel_call(
        inside_back,
        [out((rows, width), bf16), out((rows, 2 * state), bf16), out((8, mixed), f32)],
        conv, cum, cum_t, skip, dy, full, ends, pre,
    )
    after = lax.ppermute(head, "tm", down)
    pair = (pair[:quarter] + crossed.astype(f32)).astype(bf16)
    pieces = lax.all_to_all(pair.reshape(half, -1, width), "stream", 0, 0, axis_index_groups=cores)
    gp, result = kernel_call(
        conv_grad,
        [out((rows, mixed), bf16), out((block, model), bf16)],
        conv, cum, full, ends, leaving, dy, dx, dbc, pre, parts, factors,
        scalars=at,
    )
    *token_parts, own_dw = kernel_call(
        token_grad,
        [out((block, model), bf16)] + [out((block + 8, model), bf16)] * (XS - 1)
        + [out((8, width), f32)],
        gp, after, taps, dgate, w_gate, w_mix, pieces,
        scalars=at,
        scratch=[pltpu.VMEM((rows + 8, mixed), f32), pltpu.VMEM((rows, mixed), bf16),
                 pltpu.VMEM((XS, 8, model), f32)],
    )
    moved = {}
    for r in (2, 1, 3):
        moved[r] = along_x(token_parts[r], r)
    scale = (stream * tm * block) ** (-0.5)
    grad_tokens, grad_out_t = kernel_call(
        functools.partial(finish, scale),
        [out((block, model), bf16), out((3, inner), f32)],
        token_parts[0], own_dw, moved[1], moved[2], moved[3],
        scalars=at,
    )
    return (result[None], grad_tokens[None], grad_out_t)


def solution(mesh):
    data = P("stream", "tm", None)
    in_specs = (data, data, data, P("stream", None), P("stream", None), P(), P(), P())
    out_specs = (data, data, P(("tm", "stream"), None))

    return jax.shard_map(shards, mesh=mesh, in_specs=in_specs, out_specs=out_specs, check_vma=False)
```

```python
import functools

import jax
import jax.numpy as jnp
from jax import lax
from jax.experimental import pallas as pl
from jax.experimental.pallas import tpu as pltpu
from jax.sharding import PartitionSpec as P


bf16, f32 = jnp.bfloat16, jnp.float32
CHUNK = 128
LANES = 128
XS = 4
NN = (((1,), (0,)), ((), ()))
NT = (((1,), (1,)), ((), ()))
TN = (((0,), (0,)), ((), ()))


def dot(a, b, dims=NN):
    return lax.dot_general(a.astype(bf16), b.astype(bf16), dims, preferred_element_type=f32)


def exact(a, b, dims=NN):
    return lax.dot_general(
        a, b, dims, precision=lax.Precision.HIGHEST, preferred_element_type=f32
    )


def sig(v):
    return 0.5 + 0.5 * jnp.tanh(0.5 * v)


def kernel_call(body, outs, *args, scalars=None, scratch=(), flops=10**8, limit=None):
    spec = pl.BlockSpec(memory_space=pltpu.VMEM)
    size = sum(a.size * a.dtype.itemsize for a in list(args) + list(outs))
    first = [] if scalars is None else [scalars]
    return pl.pallas_call(
        body,
        out_shape=outs,
        in_specs=[pl.BlockSpec(memory_space=pltpu.SMEM)] * len(first) + [spec] * len(args),
        out_specs=[spec] * len(outs),
        scratch_shapes=list(scratch),
        compiler_params=pltpu.CompilerParams(vmem_limit_bytes=limit),
        cost_estimate=pl.CostEstimate(flops=flops, bytes_accessed=size, transcendentals=0),
    )(*first, *args)


def out(shape, dtype):
    return jax.ShapeDtypeStruct(shape, dtype)


def rows_of(c):
    return slice(c * CHUNK, (c + 1) * CHUNK)


def lanes_of(p):
    return slice(p * LANES, (p + 1) * LANES)


def halves():
    return lax.broadcasted_iota(jnp.int32, (CHUNK, LANES), 1) < LANES // 2


def causal():
    later = lax.broadcasted_iota(jnp.int32, (CHUNK, CHUNK), 0)
    return later >= lax.broadcasted_iota(jnp.int32, (CHUNK, CHUNK), 1)


def fades(cum_ref, cum_t_ref, c, head):
    column = cum_ref[rows_of(c), head * 64 : head * 64 + 1]
    row = cum_t_ref[c, head : head + 1, :]
    return jnp.where(causal(), jnp.exp(jnp.minimum(column - row, 0.0)), 0.0)


def place(at, r):
    chunk = lax.rem(at[0] + (XS - r), XS)
    return chunk, pl.ds(pl.multiple_of(chunk * CHUNK, CHUNK), CHUNK)


def prepare(at, in_w, wide, gate_w):
    width = gate_w.shape[1]
    inner = XS * width
    start = pl.multiple_of(at[0] * width, width)
    for i in range(wide.shape[0]):
        wide[i, :, :width] = in_w[:, pl.ds(inner + start, width)]
        wide[i, :, width:] = in_w[:, 2 * inner :]
    gate_w[...] = in_w[:, pl.ds(start, width)]


def pack(at, logs, tokens, halo, aux, send1, send2, send3, decays):
    block = logs.shape[1]
    step = lax.broadcasted_iota(jnp.int32, (block, block), 0)
    upto = (step <= lax.broadcasted_iota(jnp.int32, (block, block), 1)).astype(f32)
    cum = exact(jnp.log(logs[...]), upto)
    high = cum.astype(bf16).astype(f32)
    rest = cum - high
    middle = rest.astype(bf16).astype(f32)
    low = rest - middle
    per = logs.shape[0] // XS
    for j in range(XS):
        for i in range(per):
            h = j * per + i
            rows = [high[h : h + 1], middle[h : h + 1], low[h : h + 1], jnp.zeros((5, block), f32)]
            decays[j, :, i * block : (i + 1) * block] = jnp.concatenate(rows, axis=0)
    tail = halo[...].astype(f32)
    tail = jnp.where(lax.broadcasted_iota(jnp.int32, tail.shape, 0) < 3, 0.0, tail)
    aux[...] = (decays[at[0]] + tail).astype(bf16)
    for r, send in enumerate((send1, send2, send3)):
        send[:block, :] = tokens[...]
        send[block:, :] = (decays[lax.rem(at[0] + r + 1, XS)] + tail).astype(bf16)


def assemble(at, same, other, target, lanes):
    own_first = at[1] == 0
    for i in range(same.shape[0]):
        a, b = same[i, :, lanes], other[i, :, lanes]
        target[48 * i : 48 * i + 24, :] = jnp.where(own_first, a, b).astype(target.dtype)
        target[48 * i + 24 : 48 * i + 48, :] = jnp.where(own_first, b, a).astype(target.dtype)


def project(at, tokens, aux, recv1, recv2, recv3, same, other, conv_w,
            w_mix, cum, cum_t, pre, conv, states, last, mix):
    width = last.shape[1]
    chunks = XS
    block = CHUNK
    assemble(at, same, other, w_mix, slice(None))
    halo = jnp.zeros(aux.shape, f32)
    for r, source in enumerate((None, recv1, recv2, recv3)):
        c, _ = place(at, r)
        t = tokens[...] if r == 0 else source[:block, :]
        extra = (aux[...] if r == 0 else source[block:, :]).astype(f32)
        halo = halo + extra
        mix[pl.ds(pl.multiple_of(8 + c * block, 8), block), :] = (
            dot(t, w_mix[...]).astype(bf16).astype(f32)
        )
        total = extra[0:1] + extra[1:2] + extra[2:3]
        heads = [total[:, i * block : (i + 1) * block] for i in range(width // 64)]
        cum_t[c] = jnp.concatenate(heads + [jnp.zeros((8 - len(heads), block), f32)], axis=0)
    mix[:8, :] = dot(halo, w_mix[...]).astype(bf16).astype(f32)
    left = halves()
    state = jnp.zeros(last.shape, f32)
    for c in range(chunks):
        r = rows_of(c)
        square = jnp.concatenate([cum_t[c], jnp.zeros((block - 8, block), f32)], axis=0).T
        for p in range(width // LANES):
            cum[r, lanes_of(p)] = jnp.where(
                left, square[:, 2 * p : 2 * p + 1], square[:, 2 * p + 1 : 2 * p + 2]
            )
        for p in range(mix.shape[1] // LANES):
            s = lanes_of(p)
            value = jnp.zeros((CHUNK, LANES), f32)
            for k in range(4):
                start = 5 + k + c * CHUNK
                value = value + conv_w[k : k + 1, s] * mix[start : start + CHUNK, s]
            pre[r, s] = value.astype(bf16)
            conv[r, s] = (value * sig(value)).astype(bf16)
        states[c] = state.astype(bf16)
        end = cum[(c + 1) * CHUNK - 1 : (c + 1) * CHUNK, :]
        faded = jnp.exp(end - cum[r, :]) * conv[r, :width].astype(f32)
        state = jnp.exp(end) * state + dot(conv[r, width : width + 128], faded, TN)
    last[...] = state.astype(bf16)


def inside(conv, cum, cum_t, dskip, y):
    width = y.shape[1]
    left = halves()
    for c in range(y.shape[0] // CHUNK):
        r = rows_of(c)
        b, cv = conv[r, width : width + 128], conv[r, width + 128 : width + 256]
        scores = dot(cv, b, NT)
        for p in range(width // LANES):
            s = lanes_of(p)
            x = conv[r, s].astype(f32)
            weight = jnp.concatenate(
                [fades(cum, cum_t, c, 2 * p) * scores, fades(cum, cum_t, c, 2 * p + 1) * scores],
                axis=1,
            )
            both = jnp.concatenate([jnp.where(left, x, 0.0), jnp.where(left, 0.0, x)], axis=0)
            y[r, s] = (dot(weight, both) + dskip[:, s] * x).astype(y.dtype)


def gated(at, conv, cum, states, entering, y_in, tok0, tok1, tok2, tok3, cot0, cot1, cot2, cot3,
          same, other, norm_w,
          y, full, gate, dn, part, stats, w_gate, raw, w_out):
    width = y.shape[1]
    chunks = y.shape[0] // CHUNK
    assemble(at, same, other, w_gate, slice(0, width))
    for p in range(width // LANES):
        assemble(at, same, other, raw.at[p], slice(width + p * LANES, width + (p + 1) * LANES))
        for k in range(2):
            lanes = slice(k * width + p * LANES, k * width + (p + 1) * LANES)
            w_out[:, lanes] = raw[p, pl.ds(k, width, stride=2), :].astype(bf16)
    for r, (tok, cot) in enumerate(((tok0, cot0), (tok1, cot1), (tok2, cot2), (tok3, cot3))):
        here = place(at, r)[1]
        gate[here, :] = dot(tok[:CHUNK, :], w_gate[...]).astype(bf16)
        dn[here, :] = (dot(cot[...], w_out[...], NT) * norm_w[...]).astype(dn.dtype)
    carried = entering[...].astype(f32)
    ones = jnp.ones((8, LANES), f32)
    for c in range(chunks):
        r = rows_of(c)
        state = states[c].astype(f32) + carried
        full[c] = state.astype(bf16)
        carried = jnp.exp(cum[(c + 1) * CHUNK - 1 : (c + 1) * CHUNK, :]) * carried
        value = y_in[r, :].astype(f32) + jnp.exp(cum[r, :]) * dot(conv[r, width + 128 : width + 256], state)
        y[r, :] = value
        z = gate[r, :].astype(f32)
        g = value * z * sig(z)
        part[c] = dot(g * norm_w[...], w_out[...]).astype(bf16)
        squares, cross = g * g, g * dn[r, :].astype(f32)
        squares = sum(squares[:, lanes_of(p)] for p in range(width // LANES))
        cross = sum(cross[:, lanes_of(p)] for p in range(width // LANES))
        stats[0:1, r] = exact(ones, squares, NT)[0:1]
        stats[1:2, r] = exact(ones, cross, NT)[0:1]


def normed_part(inner, at, y, gate, dn, stats0, stats1, stats2, stats3, conv, cum, norm_w,
                cot0, cot1, cot2, cot3, perm,
                factors, dgate, dy, ends, first, keep, give, low, cot):
    width = y.shape[1]
    chunks = y.shape[0] // CHUNK
    adjoint = jnp.zeros(first.shape, f32)
    for c in reversed(range(chunks)):
        r = rows_of(c)
        sums = stats0[:, r] + stats1[:, r] + stats2[:, r] + stats3[:, r]
        sums = jnp.concatenate([sums, jnp.zeros((CHUNK - 2, CHUNK), f32)], axis=0).T
        factor = lax.rsqrt(sums[:, 0:1] * (1.0 / inner) + 1e-05)
        lean = factor * factor * sums[:, 1:2] * (1.0 / inner)
        factors[c] = jnp.broadcast_to(factor, (CHUNK, LANES))
        z = gate[r, :].astype(f32)
        q = sig(z)
        value = y[r, :]
        g = value * z * q
        low[r, :] = (g * factor * norm_w[...]).astype(bf16)
        dg = factor * (dn[r, :].astype(f32) - g * lean)
        dvalue = dg * z * q
        dy[r, :] = dvalue.astype(bf16)
        dgate[r, :] = (dg * value * q * (1.0 + z * (1.0 - q))).astype(bf16)
        ends[c] = adjoint.astype(bf16)
        end = cum[(c + 1) * CHUNK - 1 : (c + 1) * CHUNK, :]
        adjoint = jnp.exp(end) * adjoint + dot(
            conv[r, width + 128 : width + 256], jnp.exp(cum[r, :]) * dvalue, TN
        )
    first[...] = adjoint.astype(bf16)
    for r, source in enumerate((cot0, cot1, cot2, cot3)):
        cot[place(at, r)[1], :] = source[...]
    summed = dot(cot[...], low[...], TN)
    give[...] = dot(perm[keep.shape[0] :, :], summed).astype(bf16)
    keep[...] = dot(perm[: keep.shape[0], :], summed).astype(bf16)


def inside_back(conv, cum, cum_t, dskip, dy, full, ends, pre, dx, dbc, head):
    width = dy.shape[1]
    left = halves()
    for c in range(dy.shape[0] // CHUNK):
        r = rows_of(c)
        b, cv = conv[r, width : width + 128], conv[r, width + 128 : width + 256]
        scores = dot(cv, b, NT)
        dscores = jnp.zeros((CHUNK, CHUNK), f32)
        for p in range(width // LANES):
            s = lanes_of(p)
            x = conv[r, s]
            d = dy[r, s].astype(f32)
            da, db = jnp.where(left, d, 0.0), jnp.where(left, 0.0, d)
            fa, fb = fades(cum, cum_t, c, 2 * p), fades(cum, cum_t, c, 2 * p + 1)
            weight = jnp.concatenate([fa * scores, fb * scores], axis=0)
            dx[r, s] = (
                dot(weight, jnp.concatenate([da, db], axis=0), TN) + dskip[:, s] * d
            ).astype(dx.dtype)
            dscores = dscores + fa * dot(da, x, NT) + fb * dot(db, x, NT)
        dbc[r, :128] = dot(dscores, cv, TN).astype(dbc.dtype)
        dbc[r, 128:] = dot(dscores, b).astype(dbc.dtype)
    first = conv_rows(conv, cum, full[0], ends[0], dy, dx, dbc, pre, 0, 16)
    for lanes, value in first:
        head[:, lanes] = value[:8]


def conv_rows(conv, cum, state, adjoint, dy, dx, dbc, pre, start, count):
    width = dy.shape[1]
    r = slice(start, start + count)
    chunk_end = start // CHUNK * CHUNK + CHUNK
    fade = jnp.exp(cum[chunk_end - 1 : chunk_end, :] - cum[r, :])
    grad_x = dx[r, :] + fade * dot(conv[r, width : width + 128], adjoint)
    grad_b = dbc[r, :128] + dot(fade * conv[r, :width].astype(f32), adjoint, NT)
    grad_c = dbc[r, 128:] + dot(jnp.exp(cum[r, :]) * dy[r, :].astype(f32), state, NT)
    result = []
    for lanes, grad in (
        (slice(0, width), grad_x),
        (slice(width, width + 128), grad_b),
        (slice(width + 128, width + 256), grad_c),
    ):
        v = pre[r, lanes].astype(f32)
        q = sig(v)
        result.append((lanes, grad * q * (1.0 + v * (1.0 - q))))
    return result


def conv_grad(at, conv, cum, full, ends, leaving, dy, dx, dbc, pre, parts, factors, gp, result):
    chunks = dy.shape[0] // CHUNK
    carried = leaving[...].astype(f32)
    for c in reversed(range(chunks)):
        adjoint = ends[c].astype(f32) + carried
        end = cum[(c + 1) * CHUNK - 1 : (c + 1) * CHUNK, :]
        carried = jnp.exp(end) * carried
        rows = conv_rows(conv, cum, full[c], adjoint, dy, dx, dbc, pre, c * CHUNK, CHUNK)
        for lanes, value in rows:
            gp[rows_of(c), lanes] = value.astype(gp.dtype)
    factor = factors[at[0]]
    for p in range(result.shape[1] // LANES):
        s = lanes_of(p)
        total = sum(parts[k, :, s].astype(f32) for k in range(XS))
        result[:, s] = (total * factor).astype(bf16)


def token_grad(at, gp, after, conv_w, dgate, w_gate, w_mix, pieces,
               own, to1, to2, to3, own_dw, long, low, dws):
    rows = gp.shape[0]
    long[rows:, :] = after[...]
    for c in reversed(range(rows // CHUNK)):
        long[rows_of(c), :] = gp[rows_of(c), :].astype(f32)
        for p in range(gp.shape[1] // LANES):
            s = lanes_of(p)
            value = jnp.zeros((CHUNK, LANES), f32)
            for k in range(4):
                start = c * CHUNK + 3 - k
                value = value + conv_w[k : k + 1, s] * long[start : start + CHUNK, s]
            low[rows_of(c), s] = value.astype(bf16)
    total = sum(pieces[i].astype(f32) for i in range(pieces.shape[0]))
    width = total.shape[1]
    dws[...] = jnp.zeros(dws.shape, f32)
    for x in range(XS):
        dws[x, 0:3, :width] = total[3 * x : 3 * x + 3]
    own_dw[...] = dws[at[0], :, :width]
    for r, target in ((2, to2), (1, to1), (3, to3), (0, own)):
        c = lax.rem(at[0] + r, XS)
        here = pl.ds(pl.multiple_of(c * CHUNK, CHUNK), CHUNK)
        target[:CHUNK, :] = (
            dot(dgate[here, :], w_gate[...], NT) + dot(low[here, :], w_mix[...], NT)
        ).astype(bf16)
        if r:
            target[CHUNK:, :] = dws[c].astype(bf16)


def finish(scale, at, own, own_dw, got1, got2, got3, tokens, dw):
    width = own_dw.shape[1]
    for r, got in enumerate((own_dw, got1, got2, got3)):
        lanes = pl.ds(pl.multiple_of(place(at, r)[0] * width, width), width)
        rows = got[...] if r == 0 else got[CHUNK:, :width].astype(f32)
        dw[:, lanes] = rows[0:3] * scale
    for p in range(tokens.shape[1] // LANES):
        s = lanes_of(p)
        value = own[:, s].astype(f32)
        for got in (got1, got2, got3):
            value = value + got[:CHUNK, s].astype(f32)
        tokens[:, s] = value.astype(bf16)


def shards(tokens, cotangent, decay, in_w, out_w, conv_w, dskip, norm_w):
    tm, stream = lax.axis_size("tm"), lax.axis_size("stream")
    me_t, me_s = lax.axis_index("tm"), lax.axis_index("stream")
    mine = lax.rem(me_t, XS)
    core = lax.rem(me_s, 2)
    heads = dskip.shape[0]
    inner = norm_w.shape[0]
    model = tokens.shape[2]
    state = (in_w.shape[1] - 2 * inner) // 2
    part_heads, width = heads // XS, inner // XS
    rows = XS * tokens.shape[1]
    x_groups = [[h * XS + i for i in range(XS)] for h in range(tm // XS)]
    up = [(i, i + XS) for i in range(XS)]
    down = [(i + XS, i) for i in range(XS)]

    def own(array, axis, size):
        return lax.dynamic_slice_in_dim(array, mine * size, size, axis)

    def along_x(array, steps):
        pairs = [(h * XS + i, h * XS + (i + steps) % XS) for h in range(tm // XS) for i in range(XS)]
        return lax.ppermute(array, "tm", pairs)

    def swap_x(array):
        return lax.all_to_all(array, "tm", 0, 0, axis_index_groups=x_groups)

    cores = [[i for i in range(stream) if i % 2 == c] for c in range(2)]
    half = stream // 2

    def gather_weights(wide):
        same = lax.all_to_all(wide, "stream", 0, 0, axis_index_groups=cores)
        return same, lax.ppermute(same, "stream", [(i, i ^ 1) for i in range(stream)])

    halo = lax.ppermute(tokens[0, -8:], "tm", [(XS - 1, XS)])
    at = jnp.stack([mine, core]).astype(jnp.int32)
    block = tokens.shape[1]
    short = in_w.shape[0]
    mixed = width + 2 * state
    wide1, gate_w = kernel_call(
        prepare,
        [out((half, short, mixed), bf16), out((short, width), bf16)],
        in_w, scalars=at,
    )
    same1, other1 = gather_weights(wide1)
    aux, *sends = kernel_call(
        pack,
        [out((8, model), bf16)] + [out((block + 8, model), bf16)] * (XS - 1),
        decay[0].T, tokens[0], halo,
        scalars=at, scratch=[pltpu.VMEM((XS, 8, model), f32)],
    )
    recv, cots = [], [cotangent[0]]
    for r in range(1, XS):
        recv.append(along_x(sends[r - 1], r))
        cots.append(along_x(cotangent[0], r))
    piece = 2 * out_w.shape[0] // XS
    routes = []
    for t in range(tm):
        for s in range(stream):
            group, place_ = divmod(s, stream // XS)
            target = (t // XS * XS + group, XS * place_ + t % XS)
            routes.append((t * stream + s, target[0] * stream + target[1]))
    out_piece = lax.ppermute(own(out_w.reshape(-1, width), 0, piece), ("tm", "stream"), routes)
    wide2 = jnp.concatenate([gate_w, out_piece], axis=1)
    wide2 = jnp.broadcast_to(wide2[None], (half,) + wide2.shape)
    same2, other2 = gather_weights(wide2)

    taps = jnp.concatenate([own(conv_w[:, :inner], 1, width), conv_w[:, inner:]], axis=1)
    gain = own(norm_w, 0, width)[None]
    skip = jnp.repeat(own(dskip, 0, part_heads), width // part_heads)[None]
    index = jnp.arange(model)
    quarter = model // 4
    late, far = index // (2 * quarter), index // quarter % 2
    target = 2 * (index % quarter // (3 * XS)) + jnp.where(late == 0, core, 1 - core)
    side = me_t // XS
    target_t = index // 3 % XS + XS * jnp.where(far == 0, side, 1 - side)
    source = target_t * (3 * stream) + target * 3 + index % 3
    perm = (source[:, None] == index[None, :]).astype(bf16)

    chunks = rows // CHUNK
    w_mix, cum, cum_t, pre, conv, states, last = kernel_call(
        project,
        [out((model, mixed), bf16), out((rows, width), f32), out((chunks, 8, CHUNK), f32),
         out((rows, mixed), bf16), out((rows, mixed), bf16), out((chunks, state, width), bf16),
         out((state, width), bf16)],
        tokens[0], aux, *recv, same1, other1, taps,
        scalars=at,
        scratch=[pltpu.VMEM((rows + 8, mixed), f32)],
    )
    entering = lax.ppermute(last, "tm", up)
    (y_in,) = kernel_call(inside, [out((rows, width), f32)], conv, cum, cum_t, skip)
    y, full, gate, dn, part, stats, w_gate = kernel_call(
        gated,
        [out((rows, width), f32), out(states.shape, bf16), out((rows, width), bf16),
         out((rows, width), bf16), out((XS, block, model), bf16), out((2, rows), f32),
         out((model, width), bf16)],
        conv, cum, states, entering, y_in, tokens[0], *recv, *cots, same2, other2, gain,
        scalars=at,
        scratch=[pltpu.VMEM((width // LANES, model, LANES), f32), pltpu.VMEM((width, model), bf16)],
    )
    others = []
    for r in range(1, XS):
        others.append(along_x(stats, r))
    parts = swap_x(part)
    factors, dgate, dy, ends, first, keep, give = kernel_call(
        functools.partial(normed_part, inner),
        [out((chunks, CHUNK, LANES), f32), out((rows, width), bf16), out((rows, width), bf16),
         out(states.shape, bf16), out((state, width), bf16), out((model // 2, width), bf16),
         out((model // 2, width), bf16)],
        y, gate, dn, stats, *others, conv, cum, gain, *cots, perm,
        scalars=at,
        scratch=[pltpu.VMEM((rows, width), bf16), pltpu.VMEM((rows, model), bf16)],
    )
    leaving = lax.ppermute(first, "tm", down)
    got = lax.ppermute(give, "stream", [(i, i ^ 1) for i in range(stream)])
    pair = keep.astype(f32) + got.astype(f32)
    swap = [(i, (i + XS) % tm) for i in range(tm)]
    crossed = lax.ppermute(pair[quarter:].astype(bf16), "tm", swap)
    dx, dbc, head = kernel_call(
        inside_back,
        [out((rows, width), bf16), out((rows, 2 * state), bf16), out((8, mixed), f32)],
        conv, cum, cum_t, skip, dy, full, ends, pre,
    )
    after = lax.ppermute(head, "tm", down)
    pair = (pair[:quarter] + crossed.astype(f32)).astype(bf16)
    pieces = lax.all_to_all(pair.reshape(half, -1, width), "stream", 0, 0, axis_index_groups=cores)
    gp, result = kernel_call(
        conv_grad,
        [out((rows, mixed), bf16), out((block, model), bf16)],
        conv, cum, full, ends, leaving, dy, dx, dbc, pre, parts, factors,
        scalars=at,
    )
    *token_parts, own_dw = kernel_call(
        token_grad,
        [out((block, model), bf16)] + [out((block + 8, model), bf16)] * (XS - 1)
        + [out((8, width), f32)],
        gp, after, taps, dgate, w_gate, w_mix, pieces,
        scalars=at,
        scratch=[pltpu.VMEM((rows + 8, mixed), f32), pltpu.VMEM((rows, mixed), bf16),
                 pltpu.VMEM((XS, 8, model), f32)],
    )
    moved = {}
    for r in (2, 1, 3):
        moved[r] = along_x(token_parts[r], r)
    scale = (stream * tm * block) ** (-0.5)
    grad_tokens, grad_out_t = kernel_call(
        functools.partial(finish, scale),
        [out((block, model), bf16), out((3, inner), f32)],
        token_parts[0], own_dw, moved[1], moved[2], moved[3],
        scalars=at, limit=2**23,
    )
    return (result[None], grad_tokens[None], grad_out_t)


def solution(mesh):
    data = P("stream", "tm", None)
    in_specs = (data, data, data, P("stream", None), P("stream", None), P(), P(), P())
    out_specs = (data, data, P(("tm", "stream"), None))

    return jax.shard_map(shards, mesh=mesh, in_specs=in_specs, out_specs=out_specs, check_vma=False)
```

```python
import functools

import jax
import jax.numpy as jnp
from jax import lax
from jax.experimental import pallas as pl
from jax.experimental.pallas import tpu as pltpu
from jax.sharding import PartitionSpec as P


bf16, f32 = jnp.bfloat16, jnp.float32
CHUNK = 128
LANES = 128
XS = 4
NN = (((1,), (0,)), ((), ()))
NT = (((1,), (1,)), ((), ()))
TN = (((0,), (0,)), ((), ()))


def dot(a, b, dims=NN):
    return lax.dot_general(a.astype(bf16), b.astype(bf16), dims, preferred_element_type=f32)


def exact(a, b, dims=NN):
    return lax.dot_general(
        a, b, dims, precision=lax.Precision.HIGHEST, preferred_element_type=f32
    )


def sig(v):
    return 0.5 + 0.5 * jnp.tanh(0.5 * v)


def kernel_call(body, outs, *args, scalars=None, scratch=(), flops=10**8, limit=None):
    near = pl.BlockSpec(memory_space=pltpu.VMEM)
    size = sum(a.size * a.dtype.itemsize for a in list(args) + list(outs))
    first = [] if scalars is None else [scalars]
    return pl.pallas_call(
        body,
        out_shape=outs,
        in_specs=[pl.BlockSpec(memory_space=pltpu.SMEM)] * len(first) + [near] * len(args),
        out_specs=[near] * len(outs),
        scratch_shapes=list(scratch),
        compiler_params=pltpu.CompilerParams(vmem_limit_bytes=limit),
        cost_estimate=pl.CostEstimate(flops=flops, bytes_accessed=size, transcendentals=0),
    )(*first, *args)


def out(shape, dtype):
    return jax.ShapeDtypeStruct(shape, dtype)


def rows_of(c):
    return slice(c * CHUNK, (c + 1) * CHUNK)


def lanes_of(p):
    return slice(p * LANES, (p + 1) * LANES)


def halves():
    return lax.broadcasted_iota(jnp.int32, (CHUNK, LANES), 1) < LANES // 2


def causal():
    later = lax.broadcasted_iota(jnp.int32, (CHUNK, CHUNK), 0)
    return later >= lax.broadcasted_iota(jnp.int32, (CHUNK, CHUNK), 1)


def fades(cum_ref, cum_t_ref, c, head):
    column = cum_ref[rows_of(c), head * 64 : head * 64 + 1]
    row = cum_t_ref[c, head : head + 1, :]
    return jnp.where(causal(), jnp.exp(jnp.minimum(column - row, 0.0)), 0.0)


def place(at, r):
    chunk = lax.rem(at[0] + (XS - r), XS)
    return chunk, pl.ds(pl.multiple_of(chunk * CHUNK, CHUNK), CHUNK)


def prepare(at, in_w, wide, gate_w):
    width = gate_w.shape[1]
    inner = XS * width
    start = pl.multiple_of(at[0] * width, width)
    for i in range(wide.shape[0]):
        wide[i, :, :width] = in_w[:, pl.ds(inner + start, width)]
        wide[i, :, width:] = in_w[:, 2 * inner :]
    gate_w[...] = in_w[:, pl.ds(start, width)]


def pack(at, logs, tokens, halo, aux, send1, send2, send3, decays):
    block = logs.shape[1]
    step = lax.broadcasted_iota(jnp.int32, (block, block), 0)
    upto = (step <= lax.broadcasted_iota(jnp.int32, (block, block), 1)).astype(f32)
    cum = exact(jnp.log(logs[...]), upto)
    high = cum.astype(bf16).astype(f32)
    rest = cum - high
    middle = rest.astype(bf16).astype(f32)
    low = rest - middle
    per = logs.shape[0] // XS
    for j in range(XS):
        for i in range(per):
            h = j * per + i
            rows = [high[h : h + 1], middle[h : h + 1], low[h : h + 1], jnp.zeros((5, block), f32)]
            decays[j, :, i * block : (i + 1) * block] = jnp.concatenate(rows, axis=0)
    tail = halo[...].astype(f32)
    tail = jnp.where(lax.broadcasted_iota(jnp.int32, tail.shape, 0) < 3, 0.0, tail)
    aux[...] = (decays[at[0]] + tail).astype(bf16)
    for r, send in enumerate((send1, send2, send3)):
        send[:block, :] = tokens[...]
        send[block:, :] = (decays[lax.rem(at[0] + r + 1, XS)] + tail).astype(bf16)


def assemble(at, same, other, target, lanes):
    own_first = at[1] == 0
    for i in range(same.shape[0]):
        a, b = same[i, :, lanes], other[i, :, lanes]
        target[48 * i : 48 * i + 24, :] = jnp.where(own_first, a, b).astype(target.dtype)
        target[48 * i + 24 : 48 * i + 48, :] = jnp.where(own_first, b, a).astype(target.dtype)


def project(at, tokens, aux, recv1, recv2, recv3, same, other, conv_w,
            w_mix, cum, cum_t, pre, conv, states, last, pre0, mix):
    width = last.shape[1]
    chunks = XS
    block = CHUNK
    assemble(at, same, other, w_mix, slice(None))
    halo = jnp.zeros(aux.shape, f32)
    for r, source in enumerate((None, recv1, recv2, recv3)):
        c, _ = place(at, r)
        t = tokens[...] if r == 0 else source[:block, :]
        extra = (aux[...] if r == 0 else source[block:, :]).astype(f32)
        halo = halo + extra
        mix[pl.ds(pl.multiple_of(8 + c * block, 8), block), :] = (
            dot(t, w_mix[...]).astype(bf16).astype(f32)
        )
        total = extra[0:1] + extra[1:2] + extra[2:3]
        heads = [total[:, i * block : (i + 1) * block] for i in range(width // 64)]
        cum_t[c] = jnp.concatenate(heads + [jnp.zeros((8 - len(heads), block), f32)], axis=0)
    mix[:8, :] = dot(halo, w_mix[...]).astype(bf16).astype(f32)
    left = halves()
    state = jnp.zeros(last.shape, f32)
    for c in range(chunks):
        r = rows_of(c)
        square = jnp.concatenate([cum_t[c], jnp.zeros((block - 8, block), f32)], axis=0).T
        for p in range(width // LANES):
            cum[r, lanes_of(p)] = jnp.where(
                left, square[:, 2 * p : 2 * p + 1], square[:, 2 * p + 1 : 2 * p + 2]
            )
        for p in range(mix.shape[1] // LANES):
            s = lanes_of(p)
            value = jnp.zeros((CHUNK, LANES), f32)
            for k in range(4):
                start = 5 + k + c * CHUNK
                value = value + conv_w[k : k + 1, s] * mix[start : start + CHUNK, s]
            pre[r, s] = value.astype(bf16)
            conv[r, s] = (value * sig(value)).astype(bf16)
        states[c] = state.astype(bf16)
        end = cum[(c + 1) * CHUNK - 1 : (c + 1) * CHUNK, :]
        faded = jnp.exp(end - cum[r, :]) * conv[r, :width].astype(f32)
        state = jnp.exp(end) * state + dot(conv[r, width : width + 128], faded, TN)
    last[...] = state.astype(bf16)
    pre0[...] = pre[: pre0.shape[0], :]


def inside(conv, cum, cum_t, dskip, y):
    width = y.shape[1]
    left = halves()
    for c in range(y.shape[0] // CHUNK):
        r = rows_of(c)
        b, cv = conv[r, width : width + 128], conv[r, width + 128 : width + 256]
        scores = dot(cv, b, NT)
        for p in range(width // LANES):
            s = lanes_of(p)
            x = conv[r, s].astype(f32)
            weight = jnp.concatenate(
                [fades(cum, cum_t, c, 2 * p) * scores, fades(cum, cum_t, c, 2 * p + 1) * scores],
                axis=1,
            )
            both = jnp.concatenate([jnp.where(left, x, 0.0), jnp.where(left, 0.0, x)], axis=0)
            y[r, s] = (dot(weight, both) + dskip[:, s] * x).astype(y.dtype)


def gated(at, conv, cum, states, entering, y_in, tok0, tok1, tok2, tok3, cot0, cot1, cot2, cot3,
          same, other, norm_w,
          y, full, gate, dn, part, stats, w_gate, full0, raw, w_out):
    width = y.shape[1]
    chunks = y.shape[0] // CHUNK
    assemble(at, same, other, w_gate, slice(0, width))
    for p in range(width // LANES):
        assemble(at, same, other, raw.at[p], slice(width + p * LANES, width + (p + 1) * LANES))
        for k in range(2):
            lanes = slice(k * width + p * LANES, k * width + (p + 1) * LANES)
            w_out[:, lanes] = raw[p, pl.ds(k, width, stride=2), :].astype(bf16)
    for r, (tok, cot) in enumerate(((tok0, cot0), (tok1, cot1), (tok2, cot2), (tok3, cot3))):
        here = place(at, r)[1]
        gate[here, :] = dot(tok[:CHUNK, :], w_gate[...]).astype(bf16)
        dn[here, :] = (dot(cot[...], w_out[...], NT) * norm_w[...]).astype(dn.dtype)
    carried = entering[...].astype(f32)
    ones = jnp.ones((8, LANES), f32)
    for c in range(chunks):
        r = rows_of(c)
        state = states[c].astype(f32) + carried
        full[c] = state.astype(bf16)
        if c == 0:
            full0[...] = state.astype(bf16)
        carried = jnp.exp(cum[(c + 1) * CHUNK - 1 : (c + 1) * CHUNK, :]) * carried
        value = y_in[r, :].astype(f32) + jnp.exp(cum[r, :]) * dot(conv[r, width + 128 : width + 256], state)
        y[r, :] = value
        z = gate[r, :].astype(f32)
        g = value * z * sig(z)
        part[c] = dot(g * norm_w[...], w_out[...]).astype(bf16)
        squares, cross = g * g, g * dn[r, :].astype(f32)
        squares = sum(squares[:, lanes_of(p)] for p in range(width // LANES))
        cross = sum(cross[:, lanes_of(p)] for p in range(width // LANES))
        stats[0:1, r] = exact(ones, squares, NT)[0:1]
        stats[1:2, r] = exact(ones, cross, NT)[0:1]


def normed_part(inner, at, y, gate, dn, stats0, stats1, stats2, stats3, conv, cum, norm_w,
                cot0, cot1, cot2, cot3, perm,
                factors, dgate, dy, ends, first, keep, give, ends0, low, cot):
    width = y.shape[1]
    chunks = y.shape[0] // CHUNK
    adjoint = jnp.zeros(first.shape, f32)
    for c in reversed(range(chunks)):
        r = rows_of(c)
        sums = stats0[:, r] + stats1[:, r] + stats2[:, r] + stats3[:, r]
        sums = jnp.concatenate([sums, jnp.zeros((CHUNK - 2, CHUNK), f32)], axis=0).T
        factor = lax.rsqrt(sums[:, 0:1] * (1.0 / inner) + 1e-05)
        lean = factor * factor * sums[:, 1:2] * (1.0 / inner)
        factors[c] = jnp.broadcast_to(factor, (CHUNK, LANES))
        z = gate[r, :].astype(f32)
        q = sig(z)
        value = y[r, :]
        g = value * z * q
        low[r, :] = (g * factor * norm_w[...]).astype(bf16)
        dg = factor * (dn[r, :].astype(f32) - g * lean)
        dvalue = dg * z * q
        dy[r, :] = dvalue.astype(bf16)
        dgate[r, :] = (dg * value * q * (1.0 + z * (1.0 - q))).astype(bf16)
        ends[c] = adjoint.astype(bf16)
        if c == 0:
            ends0[...] = adjoint.astype(bf16)
        end = cum[(c + 1) * CHUNK - 1 : (c + 1) * CHUNK, :]
        adjoint = jnp.exp(end) * adjoint + dot(
            conv[r, width + 128 : width + 256], jnp.exp(cum[r, :]) * dvalue, TN
        )
    first[...] = adjoint.astype(bf16)
    for r, source in enumerate((cot0, cot1, cot2, cot3)):
        cot[place(at, r)[1], :] = source[...]
    summed = dot(cot[...], low[...], TN)
    give[...] = dot(perm[keep.shape[0] :, :], summed).astype(bf16)
    keep[...] = dot(perm[: keep.shape[0], :], summed).astype(bf16)


def inside_back(conv, cum, cum_t, dskip, dy, full0, ends0, pre, dx, dbc, head):
    width = dy.shape[1]
    left = halves()
    for c in range(dy.shape[0] // CHUNK):
        r = rows_of(c)
        b, cv = conv[r, width : width + 128], conv[r, width + 128 : width + 256]
        scores = dot(cv, b, NT)
        dscores = jnp.zeros((CHUNK, CHUNK), f32)
        for p in range(width // LANES):
            s = lanes_of(p)
            x = conv[r, s]
            d = dy[r, s].astype(f32)
            da, db = jnp.where(left, d, 0.0), jnp.where(left, 0.0, d)
            fa, fb = fades(cum, cum_t, c, 2 * p), fades(cum, cum_t, c, 2 * p + 1)
            weight = jnp.concatenate([fa * scores, fb * scores], axis=0)
            dx[r, s] = (
                dot(weight, jnp.concatenate([da, db], axis=0), TN) + dskip[:, s] * d
            ).astype(dx.dtype)
            dscores = dscores + fa * dot(da, x, NT) + fb * dot(db, x, NT)
        dbc[r, :128] = dot(dscores, cv, TN).astype(dbc.dtype)
        dbc[r, 128:] = dot(dscores, b).astype(dbc.dtype)
    first = conv_rows(conv, cum, full0[...], ends0[...], dy, dx, dbc, pre, 0, 16)
    for lanes, value in first:
        head[:, lanes] = value[:8]


def conv_rows(conv, cum, state, adjoint, dy, dx, dbc, pre, start, count):
    width = dy.shape[1]
    r = slice(start, start + count)
    chunk_end = start // CHUNK * CHUNK + CHUNK
    fade = jnp.exp(cum[chunk_end - 1 : chunk_end, :] - cum[r, :])
    grad_x = dx[r, :] + fade * dot(conv[r, width : width + 128], adjoint)
    grad_b = dbc[r, :128] + dot(fade * conv[r, :width].astype(f32), adjoint, NT)
    grad_c = dbc[r, 128:] + dot(jnp.exp(cum[r, :]) * dy[r, :].astype(f32), state, NT)
    result = []
    for lanes, grad in (
        (slice(0, width), grad_x),
        (slice(width, width + 128), grad_b),
        (slice(width + 128, width + 256), grad_c),
    ):
        v = pre[r, lanes].astype(f32)
        q = sig(v)
        result.append((lanes, grad * q * (1.0 + v * (1.0 - q))))
    return result


def conv_grad(at, conv, cum, full, ends, leaving, dy, dx, dbc, pre, parts, factors, gp, result):
    chunks = dy.shape[0] // CHUNK
    carried = leaving[...].astype(f32)
    for c in reversed(range(chunks)):
        adjoint = ends[c].astype(f32) + carried
        end = cum[(c + 1) * CHUNK - 1 : (c + 1) * CHUNK, :]
        carried = jnp.exp(end) * carried
        rows = conv_rows(conv, cum, full[c], adjoint, dy, dx, dbc, pre, c * CHUNK, CHUNK)
        for lanes, value in rows:
            gp[rows_of(c), lanes] = value.astype(gp.dtype)
    factor = factors[at[0]]
    for p in range(result.shape[1] // LANES):
        s = lanes_of(p)
        total = sum(parts[k, :, s].astype(f32) for k in range(XS))
        result[:, s] = (total * factor).astype(bf16)


def token_grad(at, gp, after, conv_w, dgate, w_gate, w_mix, pieces,
               own, to1, to2, to3, own_dw, long, low, dws):
    rows = gp.shape[0]
    long[rows:, :] = after[...]
    for c in reversed(range(rows // CHUNK)):
        long[rows_of(c), :] = gp[rows_of(c), :].astype(f32)
        for p in range(gp.shape[1] // LANES):
            s = lanes_of(p)
            value = jnp.zeros((CHUNK, LANES), f32)
            for k in range(4):
                start = c * CHUNK + 3 - k
                value = value + conv_w[k : k + 1, s] * long[start : start + CHUNK, s]
            low[rows_of(c), s] = value.astype(bf16)
    total = sum(pieces[i].astype(f32) for i in range(pieces.shape[0]))
    width = total.shape[1]
    dws[...] = jnp.zeros(dws.shape, f32)
    for x in range(XS):
        dws[x, 0:3, :width] = total[3 * x : 3 * x + 3]
    own_dw[...] = dws[at[0], :, :width]
    for r, target in ((2, to2), (1, to1), (3, to3), (0, own)):
        c = lax.rem(at[0] + r, XS)
        here = pl.ds(pl.multiple_of(c * CHUNK, CHUNK), CHUNK)
        target[:CHUNK, :] = (
            dot(dgate[here, :], w_gate[...], NT) + dot(low[here, :], w_mix[...], NT)
        ).astype(bf16)
        if r:
            target[CHUNK:, :] = dws[c].astype(bf16)


def finish(scale, at, own, own_dw, got1, got2, got3, tokens, dw):
    width = own_dw.shape[1]
    for r, got in enumerate((own_dw, got1, got2, got3)):
        lanes = pl.ds(pl.multiple_of(place(at, r)[0] * width, width), width)
        rows = got[...] if r == 0 else got[CHUNK:, :width].astype(f32)
        dw[:, lanes] = rows[0:3] * scale
    for p in range(tokens.shape[1] // LANES):
        s = lanes_of(p)
        value = own[:, s].astype(f32)
        for got in (got1, got2, got3):
            value = value + got[:CHUNK, s].astype(f32)
        tokens[:, s] = value.astype(bf16)


def shards(tokens, cotangent, decay, in_w, out_w, conv_w, dskip, norm_w):
    tm, stream = lax.axis_size("tm"), lax.axis_size("stream")
    me_t, me_s = lax.axis_index("tm"), lax.axis_index("stream")
    mine = lax.rem(me_t, XS)
    core = lax.rem(me_s, 2)
    heads = dskip.shape[0]
    inner = norm_w.shape[0]
    model = tokens.shape[2]
    state = (in_w.shape[1] - 2 * inner) // 2
    part_heads, width = heads // XS, inner // XS
    rows = XS * tokens.shape[1]
    x_groups = [[h * XS + i for i in range(XS)] for h in range(tm // XS)]
    up = [(i, i + XS) for i in range(XS)]
    down = [(i + XS, i) for i in range(XS)]

    def own(array, axis, size):
        return lax.dynamic_slice_in_dim(array, mine * size, size, axis)

    def along_x(array, steps):
        pairs = [(h * XS + i, h * XS + (i + steps) % XS) for h in range(tm // XS) for i in range(XS)]
        return lax.ppermute(array, "tm", pairs)

    def swap_x(array):
        return lax.all_to_all(array, "tm", 0, 0, axis_index_groups=x_groups)

    cores = [[i for i in range(stream) if i % 2 == c] for c in range(2)]
    half = stream // 2

    def gather_weights(wide):
        same = lax.all_to_all(wide, "stream", 0, 0, axis_index_groups=cores)
        return same, lax.ppermute(same, "stream", [(i, i ^ 1) for i in range(stream)])

    halo = lax.ppermute(tokens[0, -8:], "tm", [(XS - 1, XS)])
    at = jnp.stack([mine, core]).astype(jnp.int32)
    block = tokens.shape[1]
    short = in_w.shape[0]
    mixed = width + 2 * state
    wide1, gate_w = kernel_call(
        prepare,
        [out((half, short, mixed), bf16), out((short, width), bf16)],
        in_w, scalars=at,
    )
    same1, other1 = gather_weights(wide1)
    aux, *sends = kernel_call(
        pack,
        [out((8, model), bf16)] + [out((block + 8, model), bf16)] * (XS - 1),
        decay[0].T, tokens[0], halo,
        scalars=at, scratch=[pltpu.VMEM((XS, 8, model), f32)],
    )
    recv, cots = [], [cotangent[0]]
    for r in range(1, XS):
        recv.append(along_x(sends[r - 1], r))
        cots.append(along_x(cotangent[0], r))
    piece = out_w.shape[0] // XS
    routes = []
    for t in range(tm):
        for s in range(stream):
            group, place_ = divmod(s, stream // XS)
            target = (t // XS * XS + group, XS * place_ + t % XS)
            routes.append((t * stream + s, target[0] * stream + target[1]))
    out_piece = lax.ppermute(own(out_w, 0, piece), ("tm", "stream"), routes)
    wide2 = jnp.concatenate([gate_w, out_piece.reshape(short, width)], axis=1)
    wide2 = jnp.broadcast_to(wide2[None], (half,) + wide2.shape)
    same2, other2 = gather_weights(wide2)

    taps = jnp.concatenate([own(conv_w[:, :inner], 1, width), conv_w[:, inner:]], axis=1)
    gain = own(norm_w, 0, width)[None]
    skip = jnp.repeat(own(dskip, 0, part_heads), width // part_heads)[None]
    index = jnp.arange(model)
    quarter = model // 4
    late, far = index // (2 * quarter), index // quarter % 2
    target = 2 * (index % quarter // (3 * XS)) + jnp.where(late == 0, core, 1 - core)
    side = me_t // XS
    target_t = index // 3 % XS + XS * jnp.where(far == 0, side, 1 - side)
    source = target_t * (3 * stream) + target * 3 + index % 3
    perm = (source[:, None] == index[None, :]).astype(bf16)

    chunks = rows // CHUNK
    w_mix, cum, cum_t, pre, conv, states, last, pre0 = kernel_call(
        project,
        [out((model, mixed), bf16), out((rows, width), f32), out((chunks, 8, CHUNK), f32),
         out((rows, mixed), bf16), out((rows, mixed), bf16), out((chunks, state, width), bf16),
         out((state, width), bf16), out((16, mixed), bf16)],
        tokens[0], aux, *recv, same1, other1, taps,
        scalars=at,
        scratch=[pltpu.VMEM((rows + 8, mixed), f32)],
    )
    entering = lax.ppermute(last, "tm", up)
    (y_in,) = kernel_call(inside, [out((rows, width), f32)], conv, cum, cum_t, skip)
    y, full, gate, dn, part, stats, w_gate, full0 = kernel_call(
        gated,
        [out((rows, width), f32), out(states.shape, bf16), out((rows, width), bf16),
         out((rows, width), bf16), out((XS, block, model), bf16), out((2, rows), f32),
         out((model, width), bf16), out((state, width), bf16)],
        conv, cum, states, entering, y_in, tokens[0], *recv, *cots, same2, other2, gain,
        scalars=at,
        scratch=[pltpu.VMEM((width // LANES, model, LANES), f32), pltpu.VMEM((width, model), bf16)],
    )
    others = []
    for r in range(1, XS):
        others.append(along_x(stats, r))
    parts = swap_x(part)
    factors, dgate, dy, ends, first, keep, give, ends0 = kernel_call(
        functools.partial(normed_part, inner),
        [out((chunks, CHUNK, LANES), f32), out((rows, width), bf16), out((rows, width), bf16),
         out(states.shape, bf16), out((state, width), bf16), out((model // 2, width), bf16),
         out((model // 2, width), bf16), out((state, width), bf16)],
        y, gate, dn, stats, *others, conv, cum, gain, *cots, perm,
        scalars=at,
        scratch=[pltpu.VMEM((rows, width), bf16), pltpu.VMEM((rows, model), bf16)],
    )
    leaving = lax.ppermute(first, "tm", down)
    got = lax.ppermute(give, "stream", [(i, i ^ 1) for i in range(stream)])
    pair = keep.astype(f32) + got.astype(f32)
    swap = [(i, (i + XS) % tm) for i in range(tm)]
    crossed = lax.ppermute(pair[quarter:].astype(bf16), "tm", swap)
    dx, dbc, head = kernel_call(
        inside_back,
        [out((rows, width), bf16), out((rows, 2 * state), bf16), out((8, mixed), f32)],
        conv, cum, cum_t, skip, dy, full0, ends0, pre0,
    )
    after = lax.ppermute(head, "tm", down)
    pair = (pair[:quarter] + crossed.astype(f32)).astype(bf16)
    pieces = lax.all_to_all(pair.reshape(half, -1, width), "stream", 0, 0, axis_index_groups=cores)
    gp, result = kernel_call(
        conv_grad,
        [out((rows, mixed), bf16), out((block, model), bf16)],
        conv, cum, full, ends, leaving, dy, dx, dbc, pre, parts, factors,
        scalars=at,
    )
    *token_parts, own_dw = kernel_call(
        token_grad,
        [out((block, model), bf16)] + [out((block + 8, model), bf16)] * (XS - 1)
        + [out((8, width), f32)],
        gp, after, taps, dgate, w_gate, w_mix, pieces,
        scalars=at,
        scratch=[pltpu.VMEM((rows + 8, mixed), f32), pltpu.VMEM((rows, mixed), bf16),
                 pltpu.VMEM((XS, 8, model), f32)],
    )
    moved = {}
    for r in (2, 1, 3):
        moved[r] = along_x(token_parts[r], r)
    scale = (stream * tm * block) ** (-0.5)
    grad_tokens, grad_out_t = kernel_call(
        functools.partial(finish, scale),
        [out((block, model), bf16), out((3, inner), f32)],
        token_parts[0], own_dw, moved[1], moved[2], moved[3],
        scalars=at, limit=2**23,
    )
    return (result[None], grad_tokens[None], grad_out_t)


def solution(mesh):
    data = P("stream", "tm", None)
    in_specs = (data, data, data, P("stream", None), P("stream", None), P(), P(), P())
    out_specs = (data, data, P(("tm", "stream"), None))

    return jax.shard_map(shards, mesh=mesh, in_specs=in_specs, out_specs=out_specs, check_vma=False)
```
